512 devices in a mesh: mem: 64 (over x_lo, z, core), lat: 8 (over x_hi, y).
Axes of the slice: x: 4 (x_hi: 2, x_lo: 2; x = x_hi * 2 + x_lo), y: 4, z: 16, core: 2. Of those that a mesh axis runs over, the one named last changes fastest.
Arguments:
- background: float32 [512, 128, 2, 256], P('lat', 'mem'), may hold values from -16 to 16, as said below
- wind_east: bfloat16 [512, 256], P('lat'), may hold values from -0.8984375 to 0.8984375
- wind_north: bfloat16 [512, 256], P('lat'), may hold values from -0.8984375 to 0.8984375
- obs_index: int32 [8, 64, 1, 128], P('lat', 'mem'), may hold values from 0 to 511
- obs_value: float32 [8, 64, 1, 128], P('lat', 'mem'), may hold values from -4 to 4
- obs_scale: float32 [8, 64, 1, 128], P('lat', 'mem'), may hold values from 1 to 8
Outputs:
- analysis: float32 [512, 128, 2, 256], P('lat', 'mem')
The draws below stay inside these ranges and needn't reach their ends.
Inputs may be any that keep to these rules, and one draw needn't show every extreme that they name: `background`: Members' states.
All inputs are finite; a program needn't handle non-finite values.
Results may differ from the reference program's by a relative error of at most 0.0043.
Values may be sent and summed in bfloat16 or wider, within the bound.
A program may use at most 64 MiB of HBM per device.

```python
import math
import jax
import jax.numpy as jnp
from jax import lax

REALIZATION_TOTAL = 128
QUANTITY_TOTAL = 2
MERIDIAN_POINTS = 256
PW = 256
NOBS = 128
ROWS_DEV = 64
STEPS = 4
ITERS = 12
PARALLEL_LINES = 512
BANDS = 8
NPR = 1


def draw_background(key, part):
    key_base = jax.random.fold_in(key, 11)
    key_scale = jax.random.fold_in(key, 12)
    key_noise = jax.random.fold_in(key, 13)
    base = jnp.clip(jax.random.normal(key_base, (PARALLEL_LINES, 1, QUANTITY_TOTAL, MERIDIAN_POINTS), jnp.float32), -4.0, 4.0)
    spread = jnp.exp(jax.random.uniform(key_scale, (1, REALIZATION_TOTAL, 1, 1), jnp.float32, math.log(0.1), math.log(3.0)))
    noise = jnp.clip(jax.random.normal(key_noise, (PARALLEL_LINES, REALIZATION_TOTAL, QUANTITY_TOTAL, MERIDIAN_POINTS), jnp.float32), -4.0, 4.0)
    return base + spread * noise


def plant(entries, own_key, low, high):
    shape = entries.shape
    spot = [jax.random.randint(jax.random.fold_in(own_key, axis), (), 0, shape[axis]) for axis in range(len(shape))]
    entries = entries.at[tuple(spot)].set(low)
    longest = shape.index(max(shape))
    spot[longest] = (spot[longest] + 1) % shape[longest]
    return entries.at[tuple(spot)].set(high)


def shard_levels(own_key, shape, cuts, smallest, top_value):
    def one(position, shards_of):
        steps = jax.random.uniform(jax.random.fold_in(jax.random.fold_in(own_key, 6), position), (shards_of,), jnp.float32, smallest / len(cuts), top_value / len(cuts))
        return jnp.repeat(jnp.exp(steps), shape[position] // shards_of).reshape((-1,) + (1,) * (len(shape) - position - 1))

    loudness = one(*cuts[0])
    for cut in cuts[1:]:
        loudness = loudness * one(*cut)
    return loudness


def gaussian(key, shape, deviation, limit, split=(), held_as=jnp.bfloat16):
    factor_of = shard_levels(key, shape, split, -0.22, 0.18) if split else 1.0
    drawn = jax.random.normal(key, shape, jnp.float32) * deviation * factor_of
    return jnp.minimum(jnp.maximum(drawn, -limit), limit).astype(held_as)


def setup_inputs(seed: int = 0) -> dict:
    keys = jax.random.split(jax.random.key(seed), 7)
    background = draw_background(jax.random.fold_in(keys[6], 71), 0)
    wind_east = jnp.clip(jax.random.uniform(keys[1], (PARALLEL_LINES, MERIDIAN_POINTS), jnp.float32, -0.8984375, 0.8984375) * shard_levels(keys[1], (PARALLEL_LINES, MERIDIAN_POINTS), ((0, 8),), -0.4, 0.0), -0.8984375, 0.8984375).astype(jnp.bfloat16)
    wind_north = jnp.clip(jax.random.uniform(keys[2], (PARALLEL_LINES, MERIDIAN_POINTS), jnp.float32, -0.8984375, 0.8984375) * shard_levels(keys[2], (PARALLEL_LINES, MERIDIAN_POINTS), ((0, 8),), -0.4, 0.0), -0.8984375, 0.8984375).astype(jnp.bfloat16)
    obs_index = plant(jax.random.randint(keys[3], (BANDS, ROWS_DEV, NPR, NOBS), 0, QUANTITY_TOTAL * PW), jax.random.fold_in(keys[3], 1), 0, (QUANTITY_TOTAL * PW) - 1).astype(jnp.int32)
    obs_value = gaussian(keys[4], (BANDS, ROWS_DEV, NPR, NOBS), 1.0, 4.0, ((0, 8), (1, 64)), jnp.float32)
    obs_scale = jnp.clip(jnp.exp(math.log(8.0) - 2.0794415 * jax.random.uniform(keys[5], (BANDS, ROWS_DEV, NPR, NOBS), jnp.float32) ** shard_levels(keys[5], (BANDS, ROWS_DEV, NPR, NOBS), ((0, 8), (1, 64)), -0.2, 0.2)), 1.0, 8.0)
    return {"background": background, "wind_east": wind_east, "wind_north": wind_north, "obs_index": obs_index, "obs_value": obs_value, "obs_scale": obs_scale}


HIGHEST = lax.Precision.HIGHEST

def tendency(padded, circumpolar_wind_speed, poleward_wind_speed):
    center_rows = padded[1:-1]
    along_diff = jnp.roll(center_rows, -1, axis=-1) - jnp.roll(center_rows, 1, axis=-1)
    across_diff = padded[2:] - padded[:-2]
    return -0.5 * (circumpolar_wind_speed * along_diff + poleward_wind_speed * across_diff)

def predicted_realization(sample_realization, circumpolar_wind_speed, poleward_wind_speed):

    def slope(values):
        padded = jnp.pad(values, ((1, 1), (0, 0), (0, 0)))
        return tendency(padded, circumpolar_wind_speed, poleward_wind_speed)
    current = sample_realization
    for step_index in range(STEPS):
        slope_one = slope(current)
        slope_two = slope(current + 0.5 * slope_one)
        slope_three = slope(current + 0.5 * slope_two)
        slope_four = slope(current + slope_three)
        current = current + (slope_one + 2.0 * slope_two + 2.0 * slope_three + slope_four) / 6.0
    return current

def make_blocks(row_state, index_row, value_row, scale_row):
    offsets = jnp.arange(NPR, dtype=jnp.int32)[:, None] * PW
    columns = index_row // PW * MERIDIAN_POINTS + offsets + index_row % PW
    picked = jnp.take(row_state, columns.reshape(-1).astype(jnp.int32), axis=1).reshape(REALIZATION_TOTAL, NPR, NOBS)
    average = lax.optimization_barrier(jnp.mean(picked, axis=0))
    spread = (picked - average) * scale_row / math.sqrt(REALIZATION_TOTAL - 1)
    innovation = (value_row - average) * scale_row
    return jnp.concatenate([spread, innovation[None]], axis=0).astype(jnp.bfloat16)

def transform(patch_values, gram_sum):
    identity = jnp.eye(REALIZATION_TOTAL, dtype=jnp.float32)
    system = identity + gram_sum[:, :REALIZATION_TOTAL, :REALIZATION_TOTAL]
    coupling = gram_sum[:, :REALIZATION_TOTAL, REALIZATION_TOTAL]
    trace_sum = jnp.trace(system, axis1=1, axis2=2)
    scaled = system / trace_sum[:, None, None]

    def newton(turn_index, carry):
        upper_iter, lower_iter = carry
        factor = 1.5 * identity - 0.5 * jnp.einsum('pij,pjk->pik', lower_iter, upper_iter, precision=HIGHEST)
        return (jnp.einsum('pij,pjk->pik', upper_iter, factor, precision=HIGHEST), jnp.einsum('pij,pjk->pik', factor, lower_iter, precision=HIGHEST))
    start_lower = jnp.broadcast_to(identity, scaled.shape)
    upper_iter, lower_iter = lax.fori_loop(0, ITERS, newton, (scaled, start_lower))
    inv_root = lower_iter / jnp.sqrt(trace_sum)[:, None, None]
    half_step = jnp.einsum('pkl,pl->pk', inv_root, coupling, precision=HIGHEST)
    mean_weight = jnp.einsum('pkl,pl->pk', inv_root, half_step, precision=HIGHEST) / math.sqrt(REALIZATION_TOTAL - 1)
    weights = mean_weight[:, :, None] + inv_root
    center = lax.optimization_barrier(jnp.mean(patch_values, axis=0))
    return center + jnp.einsum('kfpt,pki->ifpt', patch_values - center, weights, precision=HIGHEST)

def update_with_observations(row_items):
    row_state, own_block, right_adjacent, leftward_adjacent, upper_adjacent, bottom_adjacent = row_items
    gram_sum = jnp.zeros((NPR, REALIZATION_TOTAL + 1, REALIZATION_TOTAL + 1), jnp.float32)
    for neighbor_block in (own_block, right_adjacent, leftward_adjacent, upper_adjacent, bottom_adjacent):
        widened = neighbor_block.astype(jnp.float32)
        gram_sum = gram_sum + jnp.einsum('kpj,lpj->pkl', widened, widened, precision=HIGHEST)
    result = transform(row_state.reshape(REALIZATION_TOTAL, QUANTITY_TOTAL, NPR, PW), gram_sum)
    return result.reshape(REALIZATION_TOTAL, QUANTITY_TOTAL, MERIDIAN_POINTS)

def reference(background, wind_east, wind_north, obs_index, obs_value, obs_scale):
    circumpolar_wind_speed = wind_east.astype(jnp.float32)[:, None, :]
    poleward_wind_speed = wind_north.astype(jnp.float32)[:, None, :]

    def advance(sample_realization):
        return predicted_realization(sample_realization, circumpolar_wind_speed, poleward_wind_speed)
    advanced_in_time = lax.map(advance, jnp.moveaxis(background, 1, 0))
    integrate_model = jnp.moveaxis(advanced_in_time, 0, 1)
    model_variables = integrate_model.reshape(PARALLEL_LINES, REALIZATION_TOTAL, QUANTITY_TOTAL * MERIDIAN_POINTS)
    index_rows = obs_index.reshape(PARALLEL_LINES, NPR, NOBS)
    value_rows = obs_value.reshape(PARALLEL_LINES, NPR, NOBS)
    scale_rows = obs_scale.reshape(PARALLEL_LINES, NPR, NOBS)

    def block_row(row_items):
        return make_blocks(row_items[0], row_items[1], row_items[2], row_items[3])
    mesh_tiles = lax.map(block_row, (model_variables, index_rows, value_rows, scale_rows))
    zero_row = jnp.zeros((1,) + mesh_tiles.shape[1:], jnp.bfloat16)
    upper_adjacent = jnp.concatenate([zero_row, mesh_tiles[:-1]], axis=0)
    bottom_adjacent = jnp.concatenate([mesh_tiles[1:], zero_row], axis=0)
    right_adjacent = jnp.roll(mesh_tiles, -1, axis=2)
    leftward_adjacent = jnp.roll(mesh_tiles, 1, axis=2)
    return lax.map(update_with_observations, (integrate_model, mesh_tiles, right_adjacent, leftward_adjacent, upper_adjacent, bottom_adjacent))
```

```python
import functools
import math

import jax
import jax.numpy as jnp
from jax import lax
from jax.experimental import pallas as pl
from jax.experimental.pallas import tpu as pltpu
from jax.sharding import PartitionSpec as P

PW = 256
NOBS = 128
STEPS = 4
ITERS = 12
HALO = 4 * STEPS
MESH = pl.DeviceIdType.MESH
BF = jnp.bfloat16
F32 = jnp.float32


def remote(src, dst, send, recv, lat, mem):
    return pltpu.make_async_remote_copy(
        src_ref=src,
        dst_ref=dst,
        send_sem=send,
        recv_sem=recv,
        device_id={"lat": lat, "mem": mem},
        device_id_type=MESH,
    )


def signal(sem, lat, mem):
    pl.semaphore_signal(
        sem, inc=1, device_id={"lat": lat, "mem": mem}, device_id_type=MESH
    )


def halo_kernel(rows, lats, bg, we, wn, up, dn, weu, wed, wnu, wnd, ssem, rsem):
    lat = lax.axis_index("lat")
    mem = lax.axis_index("mem")
    has_up = lat > 0
    has_dn = lat < lats - 1
    barrier = pltpu.get_barrier_semaphore()

    @pl.when(has_up)
    def _():
        signal(barrier, lat - 1, mem)

    @pl.when(has_dn)
    def _():
        signal(barrier, lat + 1, mem)

    pl.semaphore_wait(barrier, has_up.astype(jnp.int32) + has_dn.astype(jnp.int32))

    first = pl.ds(0, HALO)
    last = pl.ds(rows - HALO, HALO)

    def copies(target, at, sinks, base):
        return [
            remote(src.at[at], dst, ssem.at[base + i], rsem.at[base + i], target, mem)
            for i, (src, dst) in enumerate(zip((bg, we, wn), sinks))
        ]

    to_up = copies(lat - 1, first, (dn, wed, wnd), 0)
    to_dn = copies(lat + 1, last, (up, weu, wnu), 3)

    @pl.when(has_up)
    def _():
        for copy in to_up:
            copy.start()

    @pl.when(has_dn)
    def _():
        for copy in to_dn:
            copy.start()

    @pl.when(has_up)
    def _():
        for copy in to_up:
            copy.wait_send()
        for copy in to_dn:
            copy.wait_recv()

    @pl.when(has_dn)
    def _():
        for copy in to_dn:
            copy.wait_send()
        for copy in to_up:
            copy.wait_recv()


def swap_middle(x):
    sub = lax.broadcasted_iota(jnp.int32, x.shape, 1)
    down = pltpu.roll(x, 2, 1)
    lift = pltpu.roll(x, 6, 1)
    return jnp.where(
        (sub == 4) | (sub == 5), down, jnp.where((sub == 2) | (sub == 3), lift, x)
    )


def halves(x):
    high = x.astype(BF)
    low = (x - high.astype(F32)).astype(BF)
    return high, low


def dot(a, b):
    return lax.dot_general(a, b, (((1,), (0,)), ((), ())), preferred_element_type=F32)


def dot_nt(a, b):
    return lax.dot_general(a, b, (((1,), (1,)), ((), ())), preferred_element_type=F32)


def product(a, b):
    n = b.shape[1]
    ah, al = halves(a)
    bh, bl = halves(b)
    right = jnp.concatenate([bh, bl], axis=1)
    both = dot(jnp.concatenate([ah, al], axis=1), jnp.concatenate([right, right], axis=0))
    return both[:, :n] + both[:, n:]


def main_kernel(
    rows, lats,
    bg, up, dn, we, wn, weu, wed, wnu, wnd, idx, val, scl,
    out,
    q, ta, tb, we8, wn8, wf, rbuf, xf, bext, ub, db, xs, ys, s2buf, tbuf,
    ssem1, rsem1, ssemn, rsemn, ssem2, rsem2,
):
    members = 2 * rows
    total = rows + 2 * HALO
    lat = lax.axis_index("lat")
    mem = lax.axis_index("mem")
    place = lat * rows + mem
    last_place = lats * rows - 1
    has_prev = place > 0
    has_next = place < last_place
    prev_place = jnp.maximum(place - 1, 0)
    next_place = jnp.minimum(place + 1, last_place)
    prev_at = (prev_place // rows, prev_place % rows)
    next_at = (next_place // rows, next_place % rows)
    barrier = pltpu.get_barrier_semaphore()
    edge_prev = jnp.logical_and(mem == 0, lat > 0)
    edge_next = jnp.logical_and(mem == rows - 1, lat < lats - 1)

    def peer_of(i):
        return lax.rem(mem + i, rows)

    def greet(i, carry):
        signal(barrier, lat, peer_of(i))
        return carry

    lax.fori_loop(1, rows, greet, 0)

    @pl.when(edge_prev)
    def _():
        signal(barrier, *prev_at)

    @pl.when(edge_next)
    def _():
        signal(barrier, *next_at)

    zero_row = jnp.zeros((1, 8, 128), F32)
    for buf in (q, ta, tb):
        buf[0:1] = zero_row
        buf[total + 1 : total + 2] = zero_row
    for c in range(rows // 8):
        q[1 + HALO + 8 * c : 1 + HALO + 8 * c + 8] = swap_middle(bg[8 * c : 8 * c + 8])
    for west, wmid, weast, w8 in ((weu, we, wed, we8), (wnu, wn, wnd, wn8)):
        wf[0:HALO] = jnp.where(lat > 0, west[...].astype(F32), 0.0) * -0.5
        wf[HALO : HALO + rows] = wmid[...].astype(F32) * -0.5
        wf[HALO + rows : total] = jnp.where(lat < lats - 1, weast[...].astype(F32), 0.0) * -0.5
        low_half = lax.broadcasted_iota(jnp.int32, (8, 128), 0) < 4

        def widen(c, carry):
            for r in range(8):
                row = wf[pl.ds(8 * c + r, 1), :]
                w8[8 * c + r] = jnp.where(
                    low_half,
                    jnp.broadcast_to(row[:, :128], (8, 128)),
                    jnp.broadcast_to(row[:, 128:], (8, 128)),
                )
            return carry

        lax.fori_loop(0, total // 8, widen, 0)
    for c in range(HALO // 8):
        at = slice(8 * c, 8 * c + 8)
        q[1 + 8 * c : 9 + 8 * c] = jnp.where(lat > 0, swap_middle(up[at]), 0.0)
        base = 1 + HALO + rows + 8 * c
        q[base : base + 8] = jnp.where(lat < lats - 1, swap_middle(dn[at]), 0.0)

    lane = lax.broadcasted_iota(jnp.int32, (8, 8, 128), 2)

    def stage(src, dst, scale):
        def chunk(c, carry):
            base = 8 * c
            block = src[pl.ds(base, 10)]
            mid = block[1:9]
            other = pltpu.roll(mid, 4, 1)
            nxt = pltpu.roll(jnp.where(lane == 0, other, mid), 127, 2)
            prv = pltpu.roll(jnp.where(lane == 127, other, mid), 1, 2)
            here = pl.ds(base, 8)
            slope = we8[here] * (nxt - prv) + wn8[here] * (block[2:10] - block[0:8])
            dst[pl.ds(base + 1, 8)] = q[pl.ds(base + 1, 8)] + (
                slope if scale == 1.0 else scale * slope
            )
            return carry

        lax.fori_loop(0, total // 8, chunk, 0, unroll=2)

    def step(i, carry):
        stage(q, ta, 1.0 / 4.0)
        stage(ta, tb, 1.0 / 3.0)
        stage(tb, ta, 1.0 / 2.0)
        stage(ta, q, 1.0)
        return carry

    lax.fori_loop(0, STEPS, step, 0)
    greeted = rows - 1 + edge_prev.astype(jnp.int32) + edge_next.astype(jnp.int32)
    pl.semaphore_wait(barrier, greeted)

    def swap_slabs(source, offset, sink, ssem, rsem):
        def send(i, carry):
            to = peer_of(i)
            remote(
                source.at[offset + to], sink.at[mem], ssem.at[to], rsem.at[mem], lat, to
            ).start()
            return carry

        lax.fori_loop(1, rows, send, 0)
        sink[mem] = source[offset + mem]

        def settle(i, carry):
            peer = peer_of(i)
            remote(
                source.at[offset + peer], sink.at[peer], ssem.at[peer], rsem.at[peer], lat, peer
            ).wait()
            return carry

        lax.fori_loop(1, rows, settle, 0)

    swap_slabs(q, 1 + HALO, rbuf, ssem1, rsem1)

    xf[...] = rbuf[...].reshape(8 * rows, 128)
    parts = [
        jnp.concatenate(
            [xf[pl.ds(half * 4 + m * 2 + f, rows, stride=8), :] for f in range(2) for half in range(2)],
            axis=1,
        )
        for m in range(2)
    ]
    x = jnp.concatenate(parts, axis=0)
    ids = lax.broadcasted_iota(jnp.int32, (2 * PW, NOBS), 0)
    selector = jnp.where(ids == idx[...], 1.0, 0.0).astype(BF)
    xh = x.astype(BF)
    rest = x - xh.astype(F32)
    xm, xl = halves(rest)
    pieces = dot(jnp.concatenate([xh, xm, xl], axis=0), selector)
    projected = pieces[:members] + (
        pieces[members : 2 * members] + pieces[2 * members : 3 * members]
    )
    average = jnp.sum(projected, axis=0, keepdims=True) * (1.0 / members)
    spread = (projected - average) * (scl[...] * (1.0 / math.sqrt(members - 1)))
    innovation = (val[...] - average) * scl[...]
    bext[0:members] = spread.astype(BF)
    first = lax.broadcasted_iota(jnp.int32, (16, NOBS), 0) == 0
    bext[members : members + 16] = jnp.where(
        first, jnp.broadcast_to(innovation, (16, NOBS)), 0.0
    ).astype(BF)

    to_next = remote(bext, ub, ssemn.at[0], rsemn.at[0], *next_at)
    to_prev = remote(bext, db, ssemn.at[1], rsemn.at[1], *prev_at)

    @pl.when(has_next)
    def _():
        to_next.start()

    @pl.when(has_prev)
    def _():
        to_prev.start()

    own = 3.0 * dot_nt(bext[...], bext[0:members])
    center = jnp.sum(x, axis=0, keepdims=True) * (1.0 / members)
    deviation = x - center

    @pl.when(jnp.logical_not(has_prev))
    def _():
        ub[...] = jnp.zeros_like(ub)

    @pl.when(jnp.logical_not(has_next))
    def _():
        db[...] = jnp.zeros_like(db)

    @pl.when(has_next)
    def _():
        to_next.wait_send()
        to_prev.wait_recv()

    @pl.when(has_prev)
    def _():
        to_prev.wait_send()
        to_next.wait_recv()

    gram = own + dot_nt(ub[...], ub[0:members]) + dot_nt(db[...], db[0:members])
    coupling = gram[members : members + 8]
    square = lax.broadcasted_iota(jnp.int32, (members, members), 0)
    identity = jnp.where(
        square == lax.broadcasted_iota(jnp.int32, (members, members), 1), 1.0, 0.0
    )
    system = gram[0:members] + identity
    trace = jnp.sum(
        jnp.sum(system * identity, axis=1, keepdims=True), axis=0, keepdims=True
    )
    xs[...] = system / trace
    ys[...] = identity

    def newton(i, carry):
        upper = xs[...]
        lower = ys[...]
        factor = 1.5 * identity - 0.5 * product(lower, upper)
        xs[...] = product(upper, factor)
        ys[...] = product(factor, lower)
        return carry

    lax.fori_loop(0, ITERS, newton, 0)
    root = ys[...] / jnp.sqrt(trace)
    spun = product(root, deviation)
    half_step = product(coupling, root)
    shift = product(half_step, spun)[0:1] * (1.0 / math.sqrt(members - 1))
    result = spun + (center + shift)
    for m in range(2):
        for f in range(2):
            for half in range(2):
                column = (f * 2 + half) * 128
                xf[pl.ds(m * 4 + half * 2 + f, rows, stride=8), :] = result[
                    m * rows : (m + 1) * rows, column : column + 128
                ]
    s2buf[...] = xf[...].reshape(rows, 8, 128).astype(BF)
    swap_slabs(s2buf, 0, tbuf, ssem2, rsem2)
    out[...] = tbuf[...].astype(F32)


def per_device(rows, lats, background, wind_east, wind_north, obs_index, obs_value, obs_scale):
    members = 2 * rows
    total = rows + 2 * HALO
    bg = background.reshape(rows, 2, 2, 2, 128).transpose(0, 1, 3, 2, 4).reshape(rows, 8, 128)
    anywhere = pl.BlockSpec(memory_space=pl.ANY)
    vmem = pl.BlockSpec(memory_space=pltpu.VMEM)
    field = jax.ShapeDtypeStruct((HALO, 8, 128), F32)
    wind = jax.ShapeDtypeStruct((HALO, 256), BF)
    up, dn, weu, wed, wnu, wnd = pl.pallas_call(
        functools.partial(halo_kernel, rows, lats),
        out_shape=[field, field, wind, wind, wind, wind],
        in_specs=[anywhere] * 3,
        out_specs=[anywhere] * 6,
        scratch_shapes=[pltpu.SemaphoreType.DMA((6,)), pltpu.SemaphoreType.DMA((6,))],
        compiler_params=pltpu.CompilerParams(collective_id=0, has_side_effects=True),
        name="halo",
    )(bg, wind_east, wind_north)
    grid_buf = pltpu.VMEM((total + 2, 8, 128), F32)
    wide = pltpu.VMEM((total, 8, 128), F32)
    slabs = pltpu.VMEM((rows, 8, 128), BF)
    block = pltpu.VMEM((members + 16, NOBS), BF)
    square = pltpu.VMEM((members, members), F32)
    dma = pltpu.SemaphoreType.DMA
    out = pl.pallas_call(
        functools.partial(main_kernel, rows, lats),
        out_shape=jax.ShapeDtypeStruct((rows, 8, 128), F32),
        in_specs=[vmem] * 12,
        out_specs=vmem,
        scratch_shapes=[
            grid_buf, grid_buf, grid_buf, wide, wide, pltpu.VMEM((total, 256), F32),
            pltpu.VMEM((rows, 8, 128), F32), pltpu.VMEM((8 * rows, 128), F32), block, block, block,
            square, square, slabs, slabs,
            dma((rows,)), dma((rows,)), dma((2,)), dma((2,)), dma((rows,)), dma((rows,)),
        ],
        compiler_params=pltpu.CompilerParams(collective_id=1, has_side_effects=True),
        name="main",
    )(
        bg, up, dn, wind_east, wind_north, weu, wed, wnu, wnd,
        obs_index.reshape(1, NOBS), obs_value.reshape(1, NOBS), obs_scale.reshape(1, NOBS),
    )
    return out.reshape(rows, 2, 2, 2, 128).transpose(0, 1, 3, 2, 4).reshape(rows, 2, 2, 256)


def solution(mesh):
    in_specs = (
        P("lat", "mem", None, None),
        P("lat", None),
        P("lat", None),
        P("lat", "mem", None, None),
        P("lat", "mem", None, None),
        P("lat", "mem", None, None),
    )
    return jax.shard_map(
        functools.partial(per_device, mesh.shape["mem"], mesh.shape["lat"]),
        mesh=mesh,
        in_specs=in_specs,
        out_specs=P("lat", "mem", None, None),
        check_vma=False,
    )
```

```python
import functools
import math

import jax
import jax.numpy as jnp
from jax import lax
from jax.experimental import pallas as pl
from jax.experimental.pallas import tpu as pltpu
from jax.sharding import PartitionSpec as P

PW = 256
NOBS = 128
STEPS = 4
ITERS = 12
HALO = 4 * STEPS
MESH = pl.DeviceIdType.MESH
BF = jnp.bfloat16
F32 = jnp.float32


def remote(src, dst, send, recv, lat, mem):
    return pltpu.make_async_remote_copy(
        src_ref=src,
        dst_ref=dst,
        send_sem=send,
        recv_sem=recv,
        device_id={"lat": lat, "mem": mem},
        device_id_type=MESH,
    )


def signal(sem, lat, mem):
    pl.semaphore_signal(
        sem, inc=1, device_id={"lat": lat, "mem": mem}, device_id_type=MESH
    )


def swap_middle(x):
    sub = lax.broadcasted_iota(jnp.int32, x.shape, 1)
    down = pltpu.roll(x, 2, 1)
    lift = pltpu.roll(x, 6, 1)
    return jnp.where(
        (sub == 4) | (sub == 5), down, jnp.where((sub == 2) | (sub == 3), lift, x)
    )


def halves(x):
    high = x.astype(BF)
    low = (x - high.astype(F32)).astype(BF)
    return high, low


def dot(a, b):
    return lax.dot_general(a, b, (((1,), (0,)), ((), ())), preferred_element_type=F32)


def dot_nt(a, b):
    return lax.dot_general(a, b, (((1,), (1,)), ((), ())), preferred_element_type=F32)


def product(a, b):
    n = b.shape[1]
    ah, al = halves(a)
    bh, bl = halves(b)
    right = jnp.concatenate([bh, bl], axis=1)
    both = dot(jnp.concatenate([ah, al], axis=1), jnp.concatenate([right, right], axis=0))
    return both[:, :n] + both[:, n:]


def main_kernel(
    rows, lats,
    bg_in, we_in, wn_in, idx_in, val_in, scl_in,
    out,
    bg, we, wn, idx, val, scl, up, dn, weu, wed, wnu, wnd,
    q, ta, tb, we8, wn8, wfe, wfn, rbuf, xf, bext, ub, db, xs, ys, s2buf,
    lsem, hsend, hrecv, rounds, ssem1, rsem1, ssemn, rsemn, ssem2, rsem2,
):
    members = 2 * rows
    total = rows + 2 * HALO
    lat = lax.axis_index("lat")
    mem = lax.axis_index("mem")
    place = lat * rows + mem
    last_place = lats * rows - 1
    has_prev = place > 0
    has_next = place < last_place
    prev_place = jnp.maximum(place - 1, 0)
    next_place = jnp.minimum(place + 1, last_place)
    prev_at = (prev_place // rows, prev_place % rows)
    next_at = (next_place // rows, next_place % rows)
    barrier = pltpu.get_barrier_semaphore()
    edge_prev = jnp.logical_and(mem == 0, lat > 0)
    edge_next = jnp.logical_and(mem == rows - 1, lat < lats - 1)

    zs = rows // 4
    core = mem % 2
    z_here = (mem // 2) % zs
    column = mem // (rows // 2)
    starts = [
        ((column + dx) % 2) * (rows // 2) + (core + dc) % 2 for dx, dc in ((1, 1), (1, 0), (0, 1), (0, 0))
    ]

    def for_peers(act):
        def visit(z, count):
            twice = 2 * jnp.where(z >= zs, z - zs, z)
            for start in starts[:count]:
                act(start + twice)

        def pair(j, carry):
            visit(z_here + (zs // 2 - j), 4)
            visit(z_here + (zs // 2 + 1 + j), 4)
            return carry

        lax.fori_loop(0, zs // 2 - 1, pair, 0)
        visit(z_here + 1, 4)
        visit(z_here, 3)

    has_up = lat > 0
    has_dn = lat < lats - 1

    def place_at(dx, dz, dc):
        col = (column + dx) % 2
        return col * (rows // 2) + ((z_here + dz + zs) % zs) * 2 + (core + dc) % 2

    for near in ((0, 0, 1), (1, 0, 0), (0, 1, 0), (0, -1, 0)):
        signal(barrier, lat, place_at(*near))

    @pl.when(has_up)
    def _():
        signal(barrier, lat - 1, mem)

    @pl.when(has_dn)
    def _():
        signal(barrier, lat + 1, mem)

    @pl.when(edge_prev)
    def _():
        signal(barrier, *prev_at)

    @pl.when(edge_next)
    def _():
        signal(barrier, *next_at)

    local = [
        pltpu.make_async_copy(src, dst, lsem.at[i])
        for i, (src, dst) in enumerate(
            ((bg_in, bg), (we_in, we), (wn_in, wn), (idx_in, idx), (val_in, val), (scl_in, scl))
        )
    ]
    for copy in local:
        copy.start()
    greeted = 4
    for more in (has_up, has_dn, edge_prev, edge_next):
        greeted = greeted + more.astype(jnp.int32)
    pl.semaphore_wait(barrier, greeted)

    first = pl.ds(0, HALO)
    last = pl.ds(rows - HALO, HALO)

    def edge_copies(target, at, sinks, base):
        return [
            remote(src.at[at], dst, hsend.at[base + i], hrecv.at[base + i], target, mem)
            for i, (src, dst) in enumerate(zip((bg_in, we_in, wn_in), sinks))
        ]

    to_up = edge_copies(lat - 1, first, (dn, wed, wnd), 0)
    to_dn = edge_copies(lat + 1, last, (up, weu, wnu), 3)

    @pl.when(has_up)
    def _():
        for copy in to_up:
            copy.start()

    @pl.when(has_dn)
    def _():
        for copy in to_dn:
            copy.start()

    turns = [((0, 0, 1),), ((1, 0, 0),)]
    reach = 1
    while reach < zs // 2:
        turns.append(((0, reach, 0), (0, -reach, 0)))
        reach *= 2

    def tell(turn):
        for near in turns[turn]:
            signal(rounds.at[turn], lat, place_at(*near))

    def hear(turn):
        pl.semaphore_wait(rounds.at[turn], len(turns[turn]))

    tell(0)
    for copy in local:
        copy.wait()

    zero_row = jnp.zeros((1, 8, 128), F32)
    for buf in (q, ta, tb):
        buf[0:1] = zero_row
        buf[total + 1 : total + 2] = zero_row
    hear(0)
    tell(1)
    for c in range(rows // 8):
        q[1 + HALO + 8 * c : 1 + HALO + 8 * c + 8] = swap_middle(bg[8 * c : 8 * c + 8])
    hear(1)
    tell(2)
    low_half = lax.broadcasted_iota(jnp.int32, (8, 128), 0) < 4

    def spread_wind(wf, w8, start, stop):
        def widen(c, carry):
            for r in range(8):
                row = wf[pl.ds(8 * c + r, 1), :]
                w8[8 * c + r] = jnp.where(
                    low_half,
                    jnp.broadcast_to(row[:, :128], (8, 128)),
                    jnp.broadcast_to(row[:, 128:], (8, 128)),
                )
            return carry

        lax.fori_loop(start // 8, stop // 8, widen, 0)

    for wmid, w8, buf in ((we, we8, wfe), (wn, wn8, wfn)):
        buf[HALO : HALO + rows] = wmid[...].astype(F32) * -0.5
        spread_wind(buf, w8, HALO, HALO + rows)
    heard = 2
    while heard < len(turns) - 1:
        hear(heard)
        heard += 1
        tell(heard)

    @pl.when(has_up)
    def _():
        for copy in to_up:
            copy.wait_send()
        for copy in to_dn:
            copy.wait_recv()

    @pl.when(has_dn)
    def _():
        for copy in to_dn:
            copy.wait_send()
        for copy in to_up:
            copy.wait_recv()

    for west, weast, w8, buf in ((weu, wed, we8, wfe), (wnu, wnd, wn8, wfn)):
        buf[0:HALO] = jnp.where(has_up, west[...].astype(F32), 0.0) * -0.5
        buf[HALO + rows : total] = jnp.where(has_dn, weast[...].astype(F32), 0.0) * -0.5
        spread_wind(buf, w8, 0, HALO)
        spread_wind(buf, w8, HALO + rows, total)
    for c in range(HALO // 8):
        at = slice(8 * c, 8 * c + 8)
        q[1 + 8 * c : 9 + 8 * c] = jnp.where(lat > 0, swap_middle(up[at]), 0.0)
        base = 1 + HALO + rows + 8 * c
        q[base : base + 8] = jnp.where(lat < lats - 1, swap_middle(dn[at]), 0.0)

    lane = lax.broadcasted_iota(jnp.int32, (8, 8, 128), 2)

    def stage(src, dst, scale):
        def chunk(c, carry):
            base = 8 * c
            block = src[pl.ds(base, 10)]
            mid = block[1:9]
            other = pltpu.roll(mid, 4, 1)
            nxt = pltpu.roll(jnp.where(lane == 0, other, mid), 127, 2)
            prv = pltpu.roll(jnp.where(lane == 127, other, mid), 1, 2)
            here = pl.ds(base, 8)
            slope = we8[here] * (nxt - prv) + wn8[here] * (block[2:10] - block[0:8])
            dst[pl.ds(base + 1, 8)] = q[pl.ds(base + 1, 8)] + (
                slope if scale == 1.0 else scale * slope
            )
            return carry

        lax.fori_loop(0, total // 8, chunk, 0, unroll=2)

    def step(i, carry):
        stage(q, ta, 1.0 / 4.0)
        stage(ta, tb, 1.0 / 3.0)
        stage(tb, ta, 1.0 / 2.0)
        stage(ta, q, 1.0)
        return carry

    lax.fori_loop(0, STEPS, step, 0)
    hear(len(turns) - 1)

    def swap_slabs(source, offset, sink, ssem, rsem):
        def send(to):
            remote(
                source.at[offset + to], sink.at[mem], ssem.at[to], rsem.at[mem], lat, to
            ).start()

        def settle(peer):
            remote(
                source.at[offset + peer], sink.at[peer], ssem.at[peer], rsem.at[peer], lat, peer
            ).wait()

        for_peers(send)
        sink[mem] = source[offset + mem]
        for_peers(settle)

    swap_slabs(q, 1 + HALO, rbuf, ssem1, rsem1)

    xf[...] = rbuf[...].reshape(8 * rows, 128)
    parts = [
        jnp.concatenate(
            [xf[pl.ds(half * 4 + m * 2 + f, rows, stride=8), :] for f in range(2) for half in range(2)],
            axis=1,
        )
        for m in range(2)
    ]
    x = jnp.concatenate(parts, axis=0)
    ids = lax.broadcasted_iota(jnp.int32, (2 * PW, NOBS), 0)
    selector = jnp.where(ids == idx[...], 1.0, 0.0).astype(BF)
    xh = x.astype(BF)
    rest = x - xh.astype(F32)
    xm, xl = halves(rest)
    pieces = dot(jnp.concatenate([xh, xm, xl], axis=0), selector)
    projected = pieces[:members] + (
        pieces[members : 2 * members] + pieces[2 * members : 3 * members]
    )
    average = jnp.sum(projected, axis=0, keepdims=True) * (1.0 / members)
    spread = (projected - average) * (scl[...] * (1.0 / math.sqrt(members - 1)))
    innovation = (val[...] - average) * scl[...]
    bext[0:members] = spread.astype(BF)
    first = lax.broadcasted_iota(jnp.int32, (16, NOBS), 0) == 0
    bext[members : members + 16] = jnp.where(
        first, jnp.broadcast_to(innovation, (16, NOBS)), 0.0
    ).astype(BF)

    to_next = remote(bext, ub, ssemn.at[0], rsemn.at[0], *next_at)
    to_prev = remote(bext, db, ssemn.at[1], rsemn.at[1], *prev_at)

    @pl.when(has_next)
    def _():
        to_next.start()

    @pl.when(has_prev)
    def _():
        to_prev.start()

    own = 3.0 * dot_nt(bext[...], bext[0:members])
    center = jnp.sum(x, axis=0, keepdims=True) * (1.0 / members)
    deviation = x - center

    @pl.when(jnp.logical_not(has_prev))
    def _():
        ub[...] = jnp.zeros_like(ub)

    @pl.when(jnp.logical_not(has_next))
    def _():
        db[...] = jnp.zeros_like(db)

    @pl.when(has_next)
    def _():
        to_next.wait_send()
        to_prev.wait_recv()

    @pl.when(has_prev)
    def _():
        to_prev.wait_send()
        to_next.wait_recv()

    gram = own + dot_nt(ub[...], ub[0:members]) + dot_nt(db[...], db[0:members])
    coupling = gram[members : members + 8]
    square = lax.broadcasted_iota(jnp.int32, (members, members), 0)
    identity = jnp.where(
        square == lax.broadcasted_iota(jnp.int32, (members, members), 1), 1.0, 0.0
    )
    system = gram[0:members] + identity
    trace = jnp.sum(
        jnp.sum(system * identity, axis=1, keepdims=True), axis=0, keepdims=True
    )
    xs[...] = system / trace
    ys[...] = identity

    def newton(i, carry):
        upper = xs[...]
        lower = ys[...]
        factor = 1.5 * identity - 0.5 * product(lower, upper)
        xs[...] = product(upper, factor)
        ys[...] = product(factor, lower)
        return carry

    lax.fori_loop(0, ITERS, newton, 0)
    root = ys[...] / jnp.sqrt(trace)
    spun = product(root, deviation)
    half_step = product(coupling, root)
    shift = product(half_step, spun)[0:1] * (1.0 / math.sqrt(members - 1))
    result = spun + (center + shift)
    for m in range(2):
        for f in range(2):
            for half in range(2):
                column = (f * 2 + half) * 128
                xf[pl.ds(m * 4 + half * 2 + f, rows, stride=8), :] = result[
                    m * rows : (m + 1) * rows, column : column + 128
                ]
    s2buf[...] = xf[...].reshape(rows, 8, 128).astype(BF)
    swap_slabs(s2buf, 0, out, ssem2, rsem2)


def per_device(rows, lats, background, wind_east, wind_north, obs_index, obs_value, obs_scale):
    members = 2 * rows
    total = rows + 2 * HALO
    bg = background.reshape(rows, 2, 2, 2, 128).transpose(0, 1, 3, 2, 4).reshape(rows, 8, 128)
    anywhere = pl.BlockSpec(memory_space=pl.ANY)
    vmem = pl.BlockSpec(memory_space=pltpu.VMEM)
    grid_buf = pltpu.VMEM((total + 2, 8, 128), F32)
    wide = pltpu.VMEM((total, 8, 128), F32)
    grid_wind = pltpu.VMEM((total, 256), F32)
    slabs = pltpu.VMEM((rows, 8, 128), BF)
    block = pltpu.VMEM((members + 16, NOBS), BF)
    square = pltpu.VMEM((members, members), F32)
    dma = pltpu.SemaphoreType.DMA
    out = pl.pallas_call(
        functools.partial(main_kernel, rows, lats),
        out_shape=jax.ShapeDtypeStruct((rows, 8, 128), BF),
        in_specs=[anywhere] * 6,
        out_specs=vmem,
        scratch_shapes=[
            pltpu.VMEM((rows, 8, 128), F32), pltpu.VMEM((rows, 256), BF), pltpu.VMEM((rows, 256), BF),
            pltpu.VMEM((1, NOBS), jnp.int32), pltpu.VMEM((1, NOBS), F32), pltpu.VMEM((1, NOBS), F32),
            pltpu.VMEM((HALO, 8, 128), F32), pltpu.VMEM((HALO, 8, 128), F32),
            *[pltpu.VMEM((HALO, 256), BF)] * 4,
            grid_buf, grid_buf, grid_buf, wide, wide, grid_wind, grid_wind,
            pltpu.VMEM((rows, 8, 128), F32), pltpu.VMEM((8 * rows, 128), F32), block, block, block,
            square, square, slabs,
            dma((6,)), dma((6,)), dma((6,)), pltpu.SemaphoreType.REGULAR((8,)),
            dma((rows,)), dma((rows,)), dma((2,)), dma((2,)), dma((rows,)), dma((rows,)),
        ],
        compiler_params=pltpu.CompilerParams(collective_id=0, has_side_effects=True),
        name="main",
    )(
        bg, wind_east, wind_north,
        obs_index.reshape(1, NOBS), obs_value.reshape(1, NOBS), obs_scale.reshape(1, NOBS),
    )
    out = out.astype(F32)
    return out.reshape(rows, 2, 2, 2, 128).transpose(0, 1, 3, 2, 4).reshape(rows, 2, 2, 256)


def solution(mesh):
    in_specs = (
        P("lat", "mem", None, None),
        P("lat", None),
        P("lat", None),
        P("lat", "mem", None, None),
        P("lat", "mem", None, None),
        P("lat", "mem", None, None),
    )
    return jax.shard_map(
        functools.partial(per_device, mesh.shape["mem"], mesh.shape["lat"]),
        mesh=mesh,
        in_specs=in_specs,
        out_specs=P("lat", "mem", None, None),
        check_vma=False,
    )
```

```python
import functools
import math

import jax
import jax.numpy as jnp
from jax import lax
from jax.experimental import pallas as pl
from jax.experimental.pallas import tpu as pltpu
from jax.sharding import PartitionSpec as P

PW = 256
NOBS = 128
STEPS = 4
ITERS = 12
HALO = 4 * STEPS
CHUNK = HALO
MESH = pl.DeviceIdType.MESH
BF = jnp.bfloat16
F32 = jnp.float32


def remote(src, dst, send, recv, lat, mem):
    return pltpu.make_async_remote_copy(
        src_ref=src,
        dst_ref=dst,
        send_sem=send,
        recv_sem=recv,
        device_id={"lat": lat, "mem": mem},
        device_id_type=MESH,
    )


def signal(sem, lat, mem):
    pl.semaphore_signal(
        sem, inc=1, device_id={"lat": lat, "mem": mem}, device_id_type=MESH
    )


def swap_middle(x):
    sub = lax.broadcasted_iota(jnp.int32, x.shape, 1)
    down = pltpu.roll(x, 2, 1)
    lift = pltpu.roll(x, 6, 1)
    return jnp.where(
        (sub == 4) | (sub == 5), down, jnp.where((sub == 2) | (sub == 3), lift, x)
    )


def halves(x):
    high = x.astype(BF)
    low = (x - high.astype(F32)).astype(BF)
    return high, low


def dot(a, b):
    return lax.dot_general(a, b, (((1,), (0,)), ((), ())), preferred_element_type=F32)


def dot_nt(a, b):
    return lax.dot_general(a, b, (((1,), (1,)), ((), ())), preferred_element_type=F32)


def product(a, b):
    n = b.shape[1]
    ah, al = halves(a)
    bh, bl = halves(b)
    right = jnp.concatenate([bh, bl], axis=1)
    both = dot(jnp.concatenate([ah, al], axis=1), jnp.concatenate([right, right], axis=0))
    return both[:, :n] + both[:, n:]


def main_kernel(
    rows, lats,
    bg_in, we_in, wn_in, idx_in, val_in, scl_in,
    out,
    bg, we, wn, idx, val, scl, up, dn, weu, wed, wnu, wnd,
    t, we8, wn8, wfe, wfn, rbuf, xf, bext, ub, db, xs, ys, s2buf,
    lsem, hsend, hrecv, rounds, ssem1, rsem1, ssemn, rsemn, ssem2, rsem2,
):
    members = 2 * rows
    total = rows + 2 * HALO
    lat = lax.axis_index("lat")
    mem = lax.axis_index("mem")
    place = lat * rows + mem
    last_place = lats * rows - 1
    has_prev = place > 0
    has_next = place < last_place
    prev_place = jnp.maximum(place - 1, 0)
    next_place = jnp.minimum(place + 1, last_place)
    prev_at = (prev_place // rows, prev_place % rows)
    next_at = (next_place // rows, next_place % rows)
    barrier = pltpu.get_barrier_semaphore()
    edge_prev = jnp.logical_and(mem == 0, lat > 0)
    edge_next = jnp.logical_and(mem == rows - 1, lat < lats - 1)

    zs = rows // 4
    core = mem % 2
    z_here = (mem // 2) % zs
    column = mem // (rows // 2)
    starts = [
        ((column + dx) % 2) * (rows // 2) + (core + dc) % 2 for dx, dc in ((1, 1), (1, 0), (0, 1), (0, 0))
    ]

    def for_peers(act):
        def visit(z, count):
            twice = 2 * jnp.where(z >= zs, z - zs, z)
            for start in starts[:count]:
                act(start + twice)

        def pair(j, carry):
            visit(z_here + (zs // 2 - j), 4)
            visit(z_here + (zs // 2 + 1 + j), 4)
            return carry

        lax.fori_loop(0, zs // 2 - 1, pair, 0)
        visit(z_here + 1, 4)
        visit(z_here, 3)

    has_up = lat > 0
    has_dn = lat < lats - 1

    def place_at(dx, dz, dc):
        col = (column + dx) % 2
        return col * (rows // 2) + ((z_here + dz + zs) % zs) * 2 + (core + dc) % 2

    for near in ((0, 0, 1), (1, 0, 0), (0, 1, 0), (0, -1, 0)):
        signal(barrier, lat, place_at(*near))

    @pl.when(has_up)
    def _():
        signal(barrier, lat - 1, mem)

    @pl.when(has_dn)
    def _():
        signal(barrier, lat + 1, mem)

    @pl.when(edge_prev)
    def _():
        signal(barrier, *prev_at)

    @pl.when(edge_next)
    def _():
        signal(barrier, *next_at)

    local = [
        pltpu.make_async_copy(src, dst, lsem.at[i])
        for i, (src, dst) in enumerate(
            ((bg_in, bg), (we_in, we), (wn_in, wn), (idx_in, idx), (val_in, val), (scl_in, scl))
        )
    ]
    for copy in local:
        copy.start()
    greeted = 4
    for more in (has_up, has_dn, edge_prev, edge_next):
        greeted = greeted + more.astype(jnp.int32)
    pl.semaphore_wait(barrier, greeted)

    first = pl.ds(0, HALO)
    last = pl.ds(rows - HALO, HALO)

    def edge_copies(target, at, sinks, base):
        return [
            remote(src.at[at], dst, hsend.at[base + i], hrecv.at[base + i], target, mem)
            for i, (src, dst) in enumerate(zip((bg_in, we_in, wn_in), sinks))
        ]

    to_up = edge_copies(lat - 1, first, (dn, wed, wnd), 0)
    to_dn = edge_copies(lat + 1, last, (up, weu, wnu), 3)

    @pl.when(has_up)
    def _():
        for copy in to_up:
            copy.start()

    @pl.when(has_dn)
    def _():
        for copy in to_dn:
            copy.start()

    turns = [((0, 0, 1),), ((1, 0, 0),)]
    reach = 1
    while reach < zs // 2:
        turns.append(((0, reach, 0), (0, -reach, 0)))
        reach *= 2

    def tell(turn):
        for near in turns[turn]:
            signal(rounds.at[turn], lat, place_at(*near))

    def hear(turn):
        pl.semaphore_wait(rounds.at[turn], len(turns[turn]))

    tell(0)
    for copy in local:
        copy.wait()

    hear(0)
    tell(1)
    for c in range(rows // 8):
        t[0, HALO + 8 * c : HALO + 8 * c + 8] = swap_middle(bg[8 * c : 8 * c + 8])
    hear(1)
    tell(2)
    low_half = lax.broadcasted_iota(jnp.int32, (8, 128), 0) < 4

    def spread_wind(wf, w8, start, stop):
        def widen(c, carry):
            for r in range(8):
                row = wf[pl.ds(8 * c + r, 1), :]
                w8[8 * c + r] = jnp.where(
                    low_half,
                    jnp.broadcast_to(row[:, :128], (8, 128)),
                    jnp.broadcast_to(row[:, 128:], (8, 128)),
                )
            return carry

        lax.fori_loop(start // 8, stop // 8, widen, 0)

    for wmid, w8, buf in ((we, we8, wfe), (wn, wn8, wfn)):
        buf[HALO : HALO + rows] = wmid[...].astype(F32) * -0.5
        spread_wind(buf, w8, HALO, HALO + rows)
    lane = lax.broadcasted_iota(jnp.int32, (CHUNK, 8, 128), 2)

    def stage(s, base, start, scale):
        block = t[s - 1, pl.ds(start - 1, CHUNK + 2)]
        mid = block[1 : CHUNK + 1]
        other = pltpu.roll(mid, 4, 1)
        nxt = pltpu.roll(jnp.where(lane == 0, other, mid), 127, 2)
        prv = pltpu.roll(jnp.where(lane == 127, other, mid), 1, 2)
        here = pl.ds(start, CHUNK)
        slope = we8[here] * (nxt - prv) + wn8[here] * (block[2 : CHUNK + 2] - block[0:CHUNK])
        t[s, here] = t[base, here] + (slope if scale == 1.0 else scale * slope)

    def inner_step(i, carry):
        for k in range(4):
            s = 4 * i + k + 1

            def chunk(c, carry, s=s, k=k):
                stage(s, 4 * i, HALO + s + CHUNK * c, 1.0 / (4 - k))
                return carry

            lax.fori_loop(0, (rows - 2 * s + CHUNK - 1) // CHUNK, chunk, 0)
        return carry

    heard = 2
    done = 0
    while heard < len(turns) - 1:
        hear(heard)
        heard += 1
        tell(heard)
        lax.fori_loop(done, done + 2 if done < STEPS else done, inner_step, 0)
        done = min(done + 2, STEPS)
    lax.fori_loop(done, STEPS, inner_step, 0)

    @pl.when(has_up)
    def _():
        for copy in to_up:
            copy.wait_send()
        for copy in to_dn:
            copy.wait_recv()

    @pl.when(has_dn)
    def _():
        for copy in to_dn:
            copy.wait_send()
        for copy in to_up:
            copy.wait_recv()

    for west, weast, w8, buf in ((weu, wed, we8, wfe), (wnu, wnd, wn8, wfn)):
        buf[0:HALO] = jnp.where(has_up, west[...].astype(F32), 0.0) * -0.5
        buf[HALO + rows : total] = jnp.where(has_dn, weast[...].astype(F32), 0.0) * -0.5
        spread_wind(buf, w8, 0, HALO)
        spread_wind(buf, w8, HALO + rows, total)
    for c in range(HALO // 8):
        at = slice(8 * c, 8 * c + 8)
        t[0, at] = jnp.where(has_up, swap_middle(up[at]), 0.0)
        below = HALO + rows + 8 * c
        t[0, below : below + 8] = jnp.where(has_dn, swap_middle(dn[at]), 0.0)

    def rim_step(i, carry):
        for k in range(4):
            s = 4 * i + k + 1
            stage(s, 4 * i, s, 1.0 / (4 - k))
            stage(s, 4 * i, total - CHUNK - s, 1.0 / (4 - k))
        return carry

    lax.fori_loop(0, STEPS, rim_step, 0)
    hear(len(turns) - 1)

    def swap_slabs(source, offset, sink, ssem, rsem):
        def send(to):
            remote(
                source.at[offset + to], sink.at[mem], ssem.at[to], rsem.at[mem], lat, to
            ).start()

        def settle(peer):
            remote(
                source.at[offset + peer], sink.at[peer], ssem.at[peer], rsem.at[peer], lat, peer
            ).wait()

        for_peers(send)
        sink[mem] = source[offset + mem]
        for_peers(settle)

    swap_slabs(t.at[4 * STEPS], HALO, rbuf, ssem1, rsem1)

    xf[...] = rbuf[...].reshape(8 * rows, 128)
    parts = [
        jnp.concatenate(
            [xf[pl.ds(half * 4 + m * 2 + f, rows, stride=8), :] for f in range(2) for half in range(2)],
            axis=1,
        )
        for m in range(2)
    ]
    x = jnp.concatenate(parts, axis=0)
    ids = lax.broadcasted_iota(jnp.int32, (2 * PW, NOBS), 0)
    selector = jnp.where(ids == idx[...], 1.0, 0.0).astype(BF)
    xh = x.astype(BF)
    rest = x - xh.astype(F32)
    xm, xl = halves(rest)
    pieces = dot(jnp.concatenate([xh, xm, xl], axis=0), selector)
    projected = pieces[:members] + (
        pieces[members : 2 * members] + pieces[2 * members : 3 * members]
    )
    average = jnp.sum(projected, axis=0, keepdims=True) * (1.0 / members)
    spread = (projected - average) * (scl[...] * (1.0 / math.sqrt(members - 1)))
    innovation = (val[...] - average) * scl[...]
    bext[0:members] = spread.astype(BF)
    first = lax.broadcasted_iota(jnp.int32, (16, NOBS), 0) == 0
    bext[members : members + 16] = jnp.where(
        first, jnp.broadcast_to(innovation, (16, NOBS)), 0.0
    ).astype(BF)

    to_next = remote(bext, ub, ssemn.at[0], rsemn.at[0], *next_at)
    to_prev = remote(bext, db, ssemn.at[1], rsemn.at[1], *prev_at)

    @pl.when(has_next)
    def _():
        to_next.start()

    @pl.when(has_prev)
    def _():
        to_prev.start()

    own = 3.0 * dot_nt(bext[...], bext[0:members])
    center = jnp.sum(x, axis=0, keepdims=True) * (1.0 / members)
    deviation = x - center

    @pl.when(jnp.logical_not(has_prev))
    def _():
        ub[...] = jnp.zeros_like(ub)

    @pl.when(jnp.logical_not(has_next))
    def _():
        db[...] = jnp.zeros_like(db)

    @pl.when(has_next)
    def _():
        to_next.wait_send()
        to_prev.wait_recv()

    @pl.when(has_prev)
    def _():
        to_prev.wait_send()
        to_next.wait_recv()

    gram = own + dot_nt(ub[...], ub[0:members]) + dot_nt(db[...], db[0:members])
    coupling = gram[members : members + 8]
    square = lax.broadcasted_iota(jnp.int32, (members, members), 0)
    identity = jnp.where(
        square == lax.broadcasted_iota(jnp.int32, (members, members), 1), 1.0, 0.0
    )
    system = gram[0:members] + identity
    trace = jnp.sum(
        jnp.sum(system * identity, axis=1, keepdims=True), axis=0, keepdims=True
    )
    xs[...] = system / trace
    ys[...] = identity

    def newton(i, carry):
        upper = xs[...]
        lower = ys[...]
        factor = 1.5 * identity - 0.5 * product(lower, upper)
        xs[...] = product(upper, factor)
        ys[...] = product(factor, lower)
        return carry

    lax.fori_loop(0, ITERS, newton, 0)
    root = ys[...] / jnp.sqrt(trace)
    spun = product(root, deviation)
    half_step = product(coupling, root)
    shift = product(half_step, spun)[0:1] * (1.0 / math.sqrt(members - 1))
    result = spun + (center + shift)
    for m in range(2):
        for f in range(2):
            for half in range(2):
                column = (f * 2 + half) * 128
                xf[pl.ds(m * 4 + half * 2 + f, rows, stride=8), :] = result[
                    m * rows : (m + 1) * rows, column : column + 128
                ]
    s2buf[...] = xf[...].reshape(rows, 8, 128).astype(BF)
    swap_slabs(s2buf, 0, out, ssem2, rsem2)


def per_device(rows, lats, background, wind_east, wind_north, obs_index, obs_value, obs_scale):
    members = 2 * rows
    total = rows + 2 * HALO
    bg = background.reshape(rows, 2, 2, 2, 128).transpose(0, 1, 3, 2, 4).reshape(rows, 8, 128)
    anywhere = pl.BlockSpec(memory_space=pl.ANY)
    vmem = pl.BlockSpec(memory_space=pltpu.VMEM)
    wide = pltpu.VMEM((total, 8, 128), F32)
    grid_wind = pltpu.VMEM((total, 256), F32)
    slabs = pltpu.VMEM((rows, 8, 128), BF)
    block = pltpu.VMEM((members + 16, NOBS), BF)
    square = pltpu.VMEM((members, members), F32)
    dma = pltpu.SemaphoreType.DMA
    out = pl.pallas_call(
        functools.partial(main_kernel, rows, lats),
        out_shape=jax.ShapeDtypeStruct((rows, 8, 128), BF),
        in_specs=[anywhere] * 6,
        out_specs=vmem,
        scratch_shapes=[
            pltpu.VMEM((rows, 8, 128), F32), pltpu.VMEM((rows, 256), BF), pltpu.VMEM((rows, 256), BF),
            pltpu.VMEM((1, NOBS), jnp.int32), pltpu.VMEM((1, NOBS), F32), pltpu.VMEM((1, NOBS), F32),
            pltpu.VMEM((HALO, 8, 128), F32), pltpu.VMEM((HALO, 8, 128), F32),
            *[pltpu.VMEM((HALO, 256), BF)] * 4,
            pltpu.VMEM((4 * STEPS + 1, total, 8, 128), F32), wide, wide, grid_wind, grid_wind,
            pltpu.VMEM((rows, 8, 128), F32), pltpu.VMEM((8 * rows, 128), F32), block, block, block,
            square, square, slabs,
            dma((6,)), dma((6,)), dma((6,)), pltpu.SemaphoreType.REGULAR((8,)),
            dma((rows,)), dma((rows,)), dma((2,)), dma((2,)), dma((rows,)), dma((rows,)),
        ],
        compiler_params=pltpu.CompilerParams(collective_id=0, has_side_effects=True),
        name="main",
    )(
        bg, wind_east, wind_north,
        obs_index.reshape(1, NOBS), obs_value.reshape(1, NOBS), obs_scale.reshape(1, NOBS),
    )
    out = out.astype(F32)
    return out.reshape(rows, 2, 2, 2, 128).transpose(0, 1, 3, 2, 4).reshape(rows, 2, 2, 256)


def solution(mesh):
    in_specs = (
        P("lat", "mem", None, None),
        P("lat", None),
        P("lat", None),
        P("lat", "mem", None, None),
        P("lat", "mem", None, None),
        P("lat", "mem", None, None),
    )
    return jax.shard_map(
        functools.partial(per_device, mesh.shape["mem"], mesh.shape["lat"]),
        mesh=mesh,
        in_specs=in_specs,
        out_specs=P("lat", "mem", None, None),
        check_vma=False,
    )
```

```python
import functools
import math

import jax
import jax.numpy as jnp
from jax import lax
from jax.experimental import pallas as pl
from jax.experimental.pallas import tpu as pltpu
from jax.sharding import PartitionSpec as P

PW = 256
NOBS = 128
STEPS = 4
ITERS = 12
HALO = 4 * STEPS
CHUNK = HALO
BOUND = 18432.0
LEVELS = 32760.0
FINE = 16384.0
SPAN = math.log(1.0 + BOUND * FINE)
I16 = jnp.int16
I32 = jnp.int32
MESH = pl.DeviceIdType.MESH
BF = jnp.bfloat16
F32 = jnp.float32


def remote(src, dst, send, recv, lat, mem):
    return pltpu.make_async_remote_copy(
        src_ref=src,
        dst_ref=dst,
        send_sem=send,
        recv_sem=recv,
        device_id={"lat": lat, "mem": mem},
        device_id_type=MESH,
    )


def signal(sem, lat, mem):
    pl.semaphore_signal(
        sem, inc=1, device_id={"lat": lat, "mem": mem}, device_id_type=MESH
    )


def swap_middle(x):
    sub = lax.broadcasted_iota(jnp.int32, x.shape, 1)
    down = pltpu.roll(x, 2, 1)
    lift = pltpu.roll(x, 6, 1)
    return jnp.where(
        (sub == 4) | (sub == 5), down, jnp.where((sub == 2) | (sub == 3), lift, x)
    )


def halves(x):
    high = x.astype(BF)
    low = (x - high.astype(F32)).astype(BF)
    return high, low


def dot(a, b):
    return lax.dot_general(a, b, (((1,), (0,)), ((), ())), preferred_element_type=F32)


def dot_nt(a, b):
    return lax.dot_general(a, b, (((1,), (1,)), ((), ())), preferred_element_type=F32)


def product(a, b):
    n = b.shape[1]
    ah, al = halves(a)
    bh, bl = halves(b)
    right = jnp.concatenate([bh, bl], axis=1)
    both = dot(jnp.concatenate([ah, al], axis=1), jnp.concatenate([right, right], axis=0))
    return both[:, :n] + both[:, n:]


def encode(x):
    level = jnp.log(1.0 + jnp.abs(x) * FINE) * (LEVELS / SPAN)
    level = jnp.round(level).astype(I32)
    return jnp.where(x < 0.0, -level, level).astype(I16)


def decode(coded):
    level = coded.astype(I32).astype(F32)
    size = (jnp.exp(jnp.abs(level) * (SPAN / LEVELS)) - 1.0) * (1.0 / FINE)
    return jnp.where(level < 0.0, -size, size)


def main_kernel(
    rows, lats,
    bg_in, we_in, wn_in, idx_in, val_in, scl_in,
    out,
    bg, we, wn, idx, val, scl, up, dn, weu, wed, wnu, wnd,
    t, we8, wn8, wfe, wfn, sbuf, rbuf, xf, bext, ub, db, xs, ys, s2buf,
    lsem, hsend, hrecv, rounds, ssem1, rsem1, ssemn, rsemn, ssem2, rsem2,
):
    members = 2 * rows
    total = rows + 2 * HALO
    lat = lax.axis_index("lat")
    mem = lax.axis_index("mem")
    place = lat * rows + mem
    last_place = lats * rows - 1
    has_prev = place > 0
    has_next = place < last_place
    prev_place = jnp.maximum(place - 1, 0)
    next_place = jnp.minimum(place + 1, last_place)
    prev_at = (prev_place // rows, prev_place % rows)
    next_at = (next_place // rows, next_place % rows)
    barrier = pltpu.get_barrier_semaphore()
    edge_prev = jnp.logical_and(mem == 0, lat > 0)
    edge_next = jnp.logical_and(mem == rows - 1, lat < lats - 1)

    zs = rows // 4
    core = mem % 2
    z_here = (mem // 2) % zs
    column = mem // (rows // 2)
    starts = [
        ((column + dx) % 2) * (rows // 2) + (core + dc) % 2 for dx, dc in ((1, 1), (1, 0), (0, 1), (0, 0))
    ]

    def for_peers(act):
        def visit(z, count):
            twice = 2 * jnp.where(z >= zs, z - zs, z)
            for start in starts[:count]:
                act(start + twice)

        def pair(j, carry):
            visit(z_here + (zs // 2 - j), 4)
            visit(z_here + (zs // 2 + 1 + j), 4)
            return carry

        lax.fori_loop(0, zs // 2 - 1, pair, 0)
        visit(z_here + 1, 4)
        visit(z_here, 3)

    has_up = lat > 0
    has_dn = lat < lats - 1

    def place_at(dx, dz, dc):
        col = (column + dx) % 2
        return col * (rows // 2) + ((z_here + dz + zs) % zs) * 2 + (core + dc) % 2

    for near in ((0, 0, 1), (1, 0, 0), (0, 1, 0), (0, -1, 0)):
        signal(barrier, lat, place_at(*near))

    @pl.when(has_up)
    def _():
        signal(barrier, lat - 1, mem)

    @pl.when(has_dn)
    def _():
        signal(barrier, lat + 1, mem)

    @pl.when(edge_prev)
    def _():
        signal(barrier, *prev_at)

    @pl.when(edge_next)
    def _():
        signal(barrier, *next_at)

    local = [
        pltpu.make_async_copy(src, dst, lsem.at[i])
        for i, (src, dst) in enumerate(
            ((bg_in, bg), (we_in, we), (wn_in, wn), (idx_in, idx), (val_in, val), (scl_in, scl))
        )
    ]
    for copy in local:
        copy.start()
    greeted = 4
    for more in (has_up, has_dn, edge_prev, edge_next):
        greeted = greeted + more.astype(jnp.int32)
    pl.semaphore_wait(barrier, greeted)

    first = pl.ds(0, HALO)
    last = pl.ds(rows - HALO, HALO)

    def edge_copies(target, at, sinks, base):
        return [
            remote(src.at[at], dst, hsend.at[base + i], hrecv.at[base + i], target, mem)
            for i, (src, dst) in enumerate(zip((bg_in, we_in, wn_in), sinks))
        ]

    to_up = edge_copies(lat - 1, first, (dn, wed, wnd), 0)
    to_dn = edge_copies(lat + 1, last, (up, weu, wnu), 3)

    @pl.when(has_up)
    def _():
        for copy in to_up:
            copy.start()

    @pl.when(has_dn)
    def _():
        for copy in to_dn:
            copy.start()

    turns = [((0, 0, 1),), ((1, 0, 0),)]
    reach = 1
    while reach < zs // 2:
        turns.append(((0, reach, 0), (0, -reach, 0)))
        reach *= 2

    def tell(turn):
        for near in turns[turn]:
            signal(rounds.at[turn], lat, place_at(*near))

    def hear(turn):
        pl.semaphore_wait(rounds.at[turn], len(turns[turn]))

    tell(0)
    for copy in local:
        copy.wait()

    hear(0)
    tell(1)
    for c in range(rows // 8):
        t[0, HALO + 8 * c : HALO + 8 * c + 8] = swap_middle(bg[8 * c : 8 * c + 8])
    hear(1)
    tell(2)
    low_half = lax.broadcasted_iota(jnp.int32, (8, 128), 0) < 4

    def spread_wind(wf, w8, start, stop):
        def widen(c, carry):
            for r in range(8):
                row = wf[pl.ds(8 * c + r, 1), :]
                w8[8 * c + r] = jnp.where(
                    low_half,
                    jnp.broadcast_to(row[:, :128], (8, 128)),
                    jnp.broadcast_to(row[:, 128:], (8, 128)),
                )
            return carry

        lax.fori_loop(start // 8, stop // 8, widen, 0)

    for wmid, w8, buf in ((we, we8, wfe), (wn, wn8, wfn)):
        buf[HALO : HALO + rows] = wmid[...].astype(F32) * -0.5
        spread_wind(buf, w8, HALO, HALO + rows)
    lane = lax.broadcasted_iota(jnp.int32, (CHUNK, 8, 128), 2)

    def stage(s, base, start, scale):
        block = t[s - 1, pl.ds(start - 1, CHUNK + 2)]
        mid = block[1 : CHUNK + 1]
        other = pltpu.roll(mid, 4, 1)
        nxt = pltpu.roll(jnp.where(lane == 0, other, mid), 127, 2)
        prv = pltpu.roll(jnp.where(lane == 127, other, mid), 1, 2)
        here = pl.ds(start, CHUNK)
        slope = we8[here] * (nxt - prv) + wn8[here] * (block[2 : CHUNK + 2] - block[0:CHUNK])
        t[s, here] = t[base, here] + (slope if scale == 1.0 else scale * slope)

    def inner_step(i, carry):
        for k in range(4):
            s = 4 * i + k + 1

            def chunk(c, carry, s=s, k=k):
                stage(s, 4 * i, HALO + s + CHUNK * c, 1.0 / (4 - k))
                return carry

            lax.fori_loop(0, (rows - 2 * s + CHUNK - 1) // CHUNK, chunk, 0)
        return carry

    heard = 2
    done = 0
    while heard < len(turns) - 1:
        hear(heard)
        heard += 1
        tell(heard)
        lax.fori_loop(done, done + 2 if done < STEPS else done, inner_step, 0)
        done = min(done + 2, STEPS)
    lax.fori_loop(done, STEPS, inner_step, 0)

    def pack(start, stop):
        def eight(c, carry):
            sbuf[pl.ds(8 * c, 8)] = encode(t[4 * STEPS, pl.ds(HALO + 8 * c, 8)])
            return carry

        lax.fori_loop(start // 8, stop // 8, eight, 0)

    if rows > 2 * HALO:
        pack(HALO, rows - HALO)

    @pl.when(has_up)
    def _():
        for copy in to_up:
            copy.wait_send()
        for copy in to_dn:
            copy.wait_recv()

    @pl.when(has_dn)
    def _():
        for copy in to_dn:
            copy.wait_send()
        for copy in to_up:
            copy.wait_recv()

    for west, weast, w8, buf in ((weu, wed, we8, wfe), (wnu, wnd, wn8, wfn)):
        buf[0:HALO] = jnp.where(has_up, west[...].astype(F32), 0.0) * -0.5
        buf[HALO + rows : total] = jnp.where(has_dn, weast[...].astype(F32), 0.0) * -0.5
        spread_wind(buf, w8, 0, HALO)
        spread_wind(buf, w8, HALO + rows, total)
    for c in range(HALO // 8):
        at = slice(8 * c, 8 * c + 8)
        t[0, at] = jnp.where(has_up, swap_middle(up[at]), 0.0)
        below = HALO + rows + 8 * c
        t[0, below : below + 8] = jnp.where(has_dn, swap_middle(dn[at]), 0.0)

    def rim_step(i, carry):
        for k in range(4):
            s = 4 * i + k + 1
            stage(s, 4 * i, s, 1.0 / (4 - k))
            stage(s, 4 * i, total - CHUNK - s, 1.0 / (4 - k))
        return carry

    lax.fori_loop(0, STEPS, rim_step, 0)
    if rows > 2 * HALO:
        pack(0, HALO)
        pack(rows - HALO, rows)
    else:
        pack(0, rows)
    hear(len(turns) - 1)

    def swap_slabs(source, sink, ssem, rsem):
        def send(to):
            remote(source.at[to], sink.at[mem], ssem.at[to], rsem.at[mem], lat, to).start()

        def settle(peer):
            remote(source.at[peer], sink.at[peer], ssem.at[peer], rsem.at[peer], lat, peer).wait()

        for_peers(send)
        sink[mem] = source[mem]
        for_peers(settle)

    swap_slabs(sbuf, rbuf, ssem1, rsem1)

    xf[...] = decode(rbuf[...]).reshape(8 * rows, 128)
    parts = [
        jnp.concatenate(
            [xf[pl.ds(half * 4 + m * 2 + f, rows, stride=8), :] for f in range(2) for half in range(2)],
            axis=1,
        )
        for m in range(2)
    ]
    x = jnp.concatenate(parts, axis=0)
    ids = lax.broadcasted_iota(jnp.int32, (2 * PW, NOBS), 0)
    selector = jnp.where(ids == idx[...], 1.0, 0.0).astype(BF)
    xh = x.astype(BF)
    rest = x - xh.astype(F32)
    xm, xl = halves(rest)
    pieces = dot(jnp.concatenate([xh, xm, xl], axis=0), selector)
    projected = pieces[:members] + (
        pieces[members : 2 * members] + pieces[2 * members : 3 * members]
    )
    average = jnp.sum(projected, axis=0, keepdims=True) * (1.0 / members)
    spread = (projected - average) * (scl[...] * (1.0 / math.sqrt(members - 1)))
    innovation = (val[...] - average) * scl[...]
    bext[0:members] = spread.astype(BF)
    first = lax.broadcasted_iota(jnp.int32, (16, NOBS), 0) == 0
    bext[members : members + 16] = jnp.where(
        first, jnp.broadcast_to(innovation, (16, NOBS)), 0.0
    ).astype(BF)

    to_next = remote(bext, ub, ssemn.at[0], rsemn.at[0], *next_at)
    to_prev = remote(bext, db, ssemn.at[1], rsemn.at[1], *prev_at)

    @pl.when(has_next)
    def _():
        to_next.start()

    @pl.when(has_prev)
    def _():
        to_prev.start()

    own = 3.0 * dot_nt(bext[...], bext[0:members])
    center = jnp.sum(x, axis=0, keepdims=True) * (1.0 / members)
    deviation = x - center

    @pl.when(jnp.logical_not(has_prev))
    def _():
        ub[...] = jnp.zeros_like(ub)

    @pl.when(jnp.logical_not(has_next))
    def _():
        db[...] = jnp.zeros_like(db)

    @pl.when(has_next)
    def _():
        to_next.wait_send()
        to_prev.wait_recv()

    @pl.when(has_prev)
    def _():
        to_prev.wait_send()
        to_next.wait_recv()

    gram = own + dot_nt(ub[...], ub[0:members]) + dot_nt(db[...], db[0:members])
    coupling = gram[members : members + 8]
    square = lax.broadcasted_iota(jnp.int32, (members, members), 0)
    identity = jnp.where(
        square == lax.broadcasted_iota(jnp.int32, (members, members), 1), 1.0, 0.0
    )
    system = gram[0:members] + identity
    trace = jnp.sum(
        jnp.sum(system * identity, axis=1, keepdims=True), axis=0, keepdims=True
    )
    start = system / trace
    factor = 1.5 * identity - 0.5 * start
    xs[...] = product(start, factor)
    ys[...] = factor

    def newton(i, carry):
        upper = xs[...]
        lower = ys[...]
        factor = 1.5 * identity - 0.5 * product(lower, upper)
        xs[...] = product(upper, factor)
        ys[...] = product(factor, lower)
        return carry

    lax.fori_loop(1, ITERS, newton, 0)
    root = ys[...] / jnp.sqrt(trace)
    spun = product(root, deviation)
    half_step = product(coupling, root)
    shift = product(half_step, spun)[0:1] * (1.0 / math.sqrt(members - 1))
    result = spun + (center + shift)
    for m in range(2):
        for f in range(2):
            for half in range(2):
                column = (f * 2 + half) * 128
                xf[pl.ds(m * 4 + half * 2 + f, rows, stride=8), :] = result[
                    m * rows : (m + 1) * rows, column : column + 128
                ]
    s2buf[...] = xf[...].reshape(rows, 8, 128).astype(BF)
    swap_slabs(s2buf, out, ssem2, rsem2)


def per_device(rows, lats, background, wind_east, wind_north, obs_index, obs_value, obs_scale):
    members = 2 * rows
    total = rows + 2 * HALO
    bg = background.reshape(rows, 2, 2, 2, 128).transpose(0, 1, 3, 2, 4).reshape(rows, 8, 128)
    anywhere = pl.BlockSpec(memory_space=pl.ANY)
    vmem = pl.BlockSpec(memory_space=pltpu.VMEM)
    wide = pltpu.VMEM((total, 8, 128), F32)
    grid_wind = pltpu.VMEM((total, 256), F32)
    slabs = pltpu.VMEM((rows, 8, 128), BF)
    block = pltpu.VMEM((members + 16, NOBS), BF)
    square = pltpu.VMEM((members, members), F32)
    dma = pltpu.SemaphoreType.DMA
    out = pl.pallas_call(
        functools.partial(main_kernel, rows, lats),
        out_shape=jax.ShapeDtypeStruct((rows, 8, 128), BF),
        in_specs=[anywhere] * 6,
        out_specs=vmem,
        scratch_shapes=[
            pltpu.VMEM((rows, 8, 128), F32), pltpu.VMEM((rows, 256), BF), pltpu.VMEM((rows, 256), BF),
            pltpu.VMEM((1, NOBS), jnp.int32), pltpu.VMEM((1, NOBS), F32), pltpu.VMEM((1, NOBS), F32),
            pltpu.VMEM((HALO, 8, 128), F32), pltpu.VMEM((HALO, 8, 128), F32),
            *[pltpu.VMEM((HALO, 256), BF)] * 4,
            pltpu.VMEM((4 * STEPS + 1, total, 8, 128), F32), wide, wide, grid_wind, grid_wind,
            pltpu.VMEM((rows, 8, 128), I16), pltpu.VMEM((rows, 8, 128), I16),
            pltpu.VMEM((8 * rows, 128), F32), block, block, block,
            square, square, slabs,
            dma((6,)), dma((6,)), dma((6,)), pltpu.SemaphoreType.REGULAR((8,)),
            dma((rows,)), dma((rows,)), dma((2,)), dma((2,)), dma((rows,)), dma((rows,)),
        ],
        compiler_params=pltpu.CompilerParams(collective_id=0, has_side_effects=True),
        name="main",
    )(
        bg, wind_east, wind_north,
        obs_index.reshape(1, NOBS), obs_value.reshape(1, NOBS), obs_scale.reshape(1, NOBS),
    )
    out = out.astype(F32)
    return out.reshape(rows, 2, 2, 2, 128).transpose(0, 1, 3, 2, 4).reshape(rows, 2, 2, 256)


def solution(mesh):
    in_specs = (
        P("lat", "mem", None, None),
        P("lat", None),
        P("lat", None),
        P("lat", "mem", None, None),
        P("lat", "mem", None, None),
        P("lat", "mem", None, None),
    )
    return jax.shard_map(
        functools.partial(per_device, mesh.shape["mem"], mesh.shape["lat"]),
        mesh=mesh,
        in_specs=in_specs,
        out_specs=P("lat", "mem", None, None),
        check_vma=False,
    )
```

```python
import functools
import math

import jax
import jax.numpy as jnp
from jax import lax
from jax.experimental import pallas as pl
from jax.experimental.pallas import tpu as pltpu
from jax.sharding import PartitionSpec as P

PW = 256
NOBS = 128
STEPS = 4
ITERS = 12
HALO = 4 * STEPS
CHUNK = HALO
BOUND = 18432.0
LEVELS = 32760.0
FINE = 16384.0
SPAN = math.log(1.0 + BOUND * FINE)
I16 = jnp.int16
I32 = jnp.int32
MESH = pl.DeviceIdType.MESH
BF = jnp.bfloat16
F32 = jnp.float32


def remote(src, dst, send, recv, lat, mem):
    return pltpu.make_async_remote_copy(
        src_ref=src,
        dst_ref=dst,
        send_sem=send,
        recv_sem=recv,
        device_id={"lat": lat, "mem": mem},
        device_id_type=MESH,
    )


def signal(sem, lat, mem):
    pl.semaphore_signal(
        sem, inc=1, device_id={"lat": lat, "mem": mem}, device_id_type=MESH
    )


def swap_middle(x):
    sub = lax.broadcasted_iota(jnp.int32, x.shape, 1)
    down = pltpu.roll(x, 2, 1)
    lift = pltpu.roll(x, 6, 1)
    return jnp.where(
        (sub == 4) | (sub == 5), down, jnp.where((sub == 2) | (sub == 3), lift, x)
    )


def halves(x):
    high = x.astype(BF)
    low = (x - high.astype(F32)).astype(BF)
    return high, low


def dot(a, b):
    return lax.dot_general(a, b, (((1,), (0,)), ((), ())), preferred_element_type=F32)


def dot_nt(a, b):
    return lax.dot_general(a, b, (((1,), (1,)), ((), ())), preferred_element_type=F32)


def product(a, b):
    n = b.shape[1]
    ah, al = halves(a)
    bh, bl = halves(b)
    right = jnp.concatenate([bh, bl], axis=1)
    both = dot(jnp.concatenate([ah, al], axis=1), jnp.concatenate([right, right], axis=0))
    return both[:, :n] + both[:, n:]


def encode(x):
    level = jnp.log(1.0 + jnp.abs(x) * FINE) * (LEVELS / SPAN)
    level = jnp.round(level).astype(I32)
    return jnp.where(x < 0.0, -level, level).astype(I16)


def decode(coded):
    level = coded.astype(I32).astype(F32)
    size = (jnp.exp(jnp.abs(level) * (SPAN / LEVELS)) - 1.0) * (1.0 / FINE)
    return jnp.where(level < 0.0, -size, size)


def main_kernel(
    rows, lats,
    bg_in, we_in, wn_in, idx_in, val_in, scl_in,
    out,
    bg, we, wn, idx, val, scl, up, dn, weu, wed, wnu, wnd,
    t, we8, wn8, wfe, wfn, sbuf, rbuf, xf, bext, ub, db, xs, ys, s2buf,
    lsem, hsend, hrecv, rounds, ssem1, rsem1, ssemn, rsemn, ssem2, rsem2,
):
    members = 2 * rows
    total = rows + 2 * HALO
    lat = lax.axis_index("lat")
    mem = lax.axis_index("mem")
    place = lat * rows + mem
    last_place = lats * rows - 1
    has_prev = place > 0
    has_next = place < last_place
    prev_place = jnp.maximum(place - 1, 0)
    next_place = jnp.minimum(place + 1, last_place)
    prev_at = (prev_place // rows, prev_place % rows)
    next_at = (next_place // rows, next_place % rows)
    barrier = pltpu.get_barrier_semaphore()
    edge_prev = jnp.logical_and(mem == 0, lat > 0)
    edge_next = jnp.logical_and(mem == rows - 1, lat < lats - 1)

    zs = rows // 4
    core = mem % 2
    z_here = (mem // 2) % zs
    column = mem // (rows // 2)
    starts = [
        ((column + dx) % 2) * (rows // 2) + (core + dc) % 2 for dx, dc in ((1, 1), (1, 0), (0, 1), (0, 0))
    ]

    def for_peers(act):
        def visit(z, count):
            twice = 2 * jnp.where(z >= zs, z - zs, z)
            for start in starts[:count]:
                act(start + twice)

        def pair(j, carry):
            visit(z_here + (zs // 2 - j), 4)
            visit(z_here + (zs // 2 + 1 + j), 4)
            return carry

        lax.fori_loop(0, zs // 2 - 1, pair, 0)
        visit(z_here + 1, 4)
        visit(z_here, 3)

    has_up = lat > 0
    has_dn = lat < lats - 1

    def place_at(dx, dz, dc):
        col = (column + dx) % 2
        return col * (rows // 2) + ((z_here + dz + zs) % zs) * 2 + (core + dc) % 2

    first_reach = 1
    near_by = [
        (dx, dz, dc)
        for dz in range(-first_reach, first_reach + 1)
        for dx in range(2)
        for dc in range(2)
        if (dx, dz, dc) != (0, 0, 0)
    ]
    for near in near_by:
        signal(barrier, lat, place_at(*near))

    @pl.when(has_up)
    def _():
        signal(barrier, lat - 1, mem)

    @pl.when(has_dn)
    def _():
        signal(barrier, lat + 1, mem)

    @pl.when(edge_prev)
    def _():
        signal(barrier, *prev_at)

    @pl.when(edge_next)
    def _():
        signal(barrier, *next_at)

    local = [
        pltpu.make_async_copy(src, dst, lsem.at[i])
        for i, (src, dst) in enumerate(
            ((bg_in, bg), (we_in, we), (wn_in, wn), (idx_in, idx), (val_in, val), (scl_in, scl))
        )
    ]
    for copy in local:
        copy.start()
    greeted = len(near_by)
    for more in (has_up, has_dn, edge_prev, edge_next):
        greeted = greeted + more.astype(jnp.int32)
    pl.semaphore_wait(barrier, greeted)

    first = pl.ds(0, HALO)
    last = pl.ds(rows - HALO, HALO)

    def edge_copies(target, at, sinks, base):
        return [
            remote(src.at[at], dst, hsend.at[base + i], hrecv.at[base + i], target, mem)
            for i, (src, dst) in enumerate(zip((bg_in, we_in, wn_in), sinks))
        ]

    to_up = edge_copies(lat - 1, first, (dn, wed, wnd), 0)
    to_dn = edge_copies(lat + 1, last, (up, weu, wnu), 3)

    @pl.when(has_up)
    def _():
        for copy in to_up:
            copy.start()

    @pl.when(has_dn)
    def _():
        for copy in to_dn:
            copy.start()

    turns = []
    reach = first_reach
    while reach < zs // 2:
        turns.append(((0, reach, 0), (0, -reach, 0)))
        reach *= 2

    def tell(turn):
        for near in turns[turn]:
            signal(rounds.at[turn], lat, place_at(*near))

    def hear(turn):
        pl.semaphore_wait(rounds.at[turn], len(turns[turn]))

    if turns:
        tell(0)
    for copy in local:
        copy.wait()

    for c in range(rows // 8):
        t[0, HALO + 8 * c : HALO + 8 * c + 8] = swap_middle(bg[8 * c : 8 * c + 8])
    low_half = lax.broadcasted_iota(jnp.int32, (8, 128), 0) < 4

    def spread_wind(wf, w8, start, stop):
        def widen(c, carry):
            for r in range(8):
                row = wf[pl.ds(8 * c + r, 1), :]
                w8[8 * c + r] = jnp.where(
                    low_half,
                    jnp.broadcast_to(row[:, :128], (8, 128)),
                    jnp.broadcast_to(row[:, 128:], (8, 128)),
                )
            return carry

        lax.fori_loop(start // 8, stop // 8, widen, 0)

    for wmid, w8, buf in ((we, we8, wfe), (wn, wn8, wfn)):
        buf[HALO : HALO + rows] = wmid[...].astype(F32) * -0.5
        spread_wind(buf, w8, HALO, HALO + rows)
    lane = lax.broadcasted_iota(jnp.int32, (CHUNK, 8, 128), 2)

    def stage(s, base, start, scale):
        block = t[s - 1, pl.ds(start - 1, CHUNK + 2)]
        mid = block[1 : CHUNK + 1]
        other = pltpu.roll(mid, 4, 1)
        nxt = pltpu.roll(jnp.where(lane == 0, other, mid), 127, 2)
        prv = pltpu.roll(jnp.where(lane == 127, other, mid), 1, 2)
        here = pl.ds(start, CHUNK)
        slope = we8[here] * (nxt - prv) + wn8[here] * (block[2 : CHUNK + 2] - block[0:CHUNK])
        t[s, here] = t[base, here] + (slope if scale == 1.0 else scale * slope)

    def inner_step(i, carry):
        for k in range(4):
            s = 4 * i + k + 1

            def chunk(c, carry, s=s, k=k):
                stage(s, 4 * i, HALO + s + CHUNK * c, 1.0 / (4 - k))
                return carry

            lax.fori_loop(0, (rows - 2 * s + CHUNK - 1) // CHUNK, chunk, 0)
        return carry

    heard = 0
    done = 0
    while heard < len(turns) - 1:
        hear(heard)
        heard += 1
        tell(heard)
        lax.fori_loop(done, done + 2 if done < STEPS else done, inner_step, 0)
        done = min(done + 2, STEPS)
    lax.fori_loop(done, STEPS, inner_step, 0)

    def pack(start, stop):
        def eight(c, carry):
            sbuf[pl.ds(8 * c, 8)] = encode(t[4 * STEPS, pl.ds(HALO + 8 * c, 8)])
            return carry

        lax.fori_loop(start // 8, stop // 8, eight, 0)

    if rows > 2 * HALO:
        pack(HALO, rows - HALO)

    @pl.when(has_up)
    def _():
        for copy in to_up:
            copy.wait_send()
        for copy in to_dn:
            copy.wait_recv()

    @pl.when(has_dn)
    def _():
        for copy in to_dn:
            copy.wait_send()
        for copy in to_up:
            copy.wait_recv()

    for west, weast, w8, buf in ((weu, wed, we8, wfe), (wnu, wnd, wn8, wfn)):
        buf[0:HALO] = jnp.where(has_up, west[...].astype(F32), 0.0) * -0.5
        buf[HALO + rows : total] = jnp.where(has_dn, weast[...].astype(F32), 0.0) * -0.5
        spread_wind(buf, w8, 0, HALO)
        spread_wind(buf, w8, HALO + rows, total)
    for c in range(HALO // 8):
        at = slice(8 * c, 8 * c + 8)
        t[0, at] = jnp.where(has_up, swap_middle(up[at]), 0.0)
        below = HALO + rows + 8 * c
        t[0, below : below + 8] = jnp.where(has_dn, swap_middle(dn[at]), 0.0)

    def rim_step(i, carry):
        for k in range(4):
            s = 4 * i + k + 1
            stage(s, 4 * i, s, 1.0 / (4 - k))
            stage(s, 4 * i, total - CHUNK - s, 1.0 / (4 - k))
        return carry

    lax.fori_loop(0, STEPS, rim_step, 0)
    if rows > 2 * HALO:
        pack(0, HALO)
        pack(rows - HALO, rows)
    else:
        pack(0, rows)
    if turns:
        hear(len(turns) - 1)

    def swap_slabs(source, sink, ssem, rsem):
        def send(to):
            remote(source.at[to], sink.at[mem], ssem.at[to], rsem.at[mem], lat, to).start()

        def settle(peer):
            remote(source.at[peer], sink.at[peer], ssem.at[peer], rsem.at[peer], lat, peer).wait()

        for_peers(send)
        own = pltpu.make_async_copy(source.at[mem], sink.at[mem], lsem.at[0])
        own.start()
        own.wait()
        for_peers(settle)

    swap_slabs(sbuf, rbuf, ssem1, rsem1)

    xf[...] = decode(rbuf[...]).reshape(8 * rows, 128)
    parts = [
        jnp.concatenate(
            [xf[pl.ds(half * 4 + m * 2 + f, rows, stride=8), :] for f in range(2) for half in range(2)],
            axis=1,
        )
        for m in range(2)
    ]
    x = jnp.concatenate(parts, axis=0)
    ids = lax.broadcasted_iota(jnp.int32, (2 * PW, NOBS), 0)
    selector = jnp.where(ids == idx[...], 1.0, 0.0).astype(BF)
    xh = x.astype(BF)
    rest = x - xh.astype(F32)
    xm, xl = halves(rest)
    pieces = dot(jnp.concatenate([xh, xm, xl], axis=0), selector)
    projected = pieces[:members] + (
        pieces[members : 2 * members] + pieces[2 * members : 3 * members]
    )
    average = jnp.sum(projected, axis=0, keepdims=True) * (1.0 / members)
    spread = (projected - average) * (scl[...] * (1.0 / math.sqrt(members - 1)))
    innovation = (val[...] - average) * scl[...]
    bext[0:members] = spread.astype(BF)
    first = lax.broadcasted_iota(jnp.int32, (16, NOBS), 0) == 0
    bext[members : members + 16] = jnp.where(
        first, jnp.broadcast_to(innovation, (16, NOBS)), 0.0
    ).astype(BF)

    to_next = remote(bext, ub, ssemn.at[0], rsemn.at[0], *next_at)
    to_prev = remote(bext, db, ssemn.at[1], rsemn.at[1], *prev_at)

    @pl.when(has_next)
    def _():
        to_next.start()

    @pl.when(has_prev)
    def _():
        to_prev.start()

    own = 3.0 * dot_nt(bext[...], bext[0:members])
    center = jnp.sum(x, axis=0, keepdims=True) * (1.0 / members)
    deviation = x - center

    @pl.when(jnp.logical_not(has_prev))
    def _():
        ub[...] = jnp.zeros_like(ub)

    @pl.when(jnp.logical_not(has_next))
    def _():
        db[...] = jnp.zeros_like(db)

    @pl.when(has_next)
    def _():
        to_next.wait_send()
        to_prev.wait_recv()

    @pl.when(has_prev)
    def _():
        to_prev.wait_send()
        to_next.wait_recv()

    gram = own + dot_nt(ub[...], ub[0:members]) + dot_nt(db[...], db[0:members])
    coupling = gram[members : members + 8]
    square = lax.broadcasted_iota(jnp.int32, (members, members), 0)
    identity = jnp.where(
        square == lax.broadcasted_iota(jnp.int32, (members, members), 1), 1.0, 0.0
    )
    system = gram[0:members] + identity
    trace = jnp.sum(
        jnp.sum(system * identity, axis=1, keepdims=True), axis=0, keepdims=True
    )
    start = system / trace
    factor = 1.5 * identity - 0.5 * start
    xs[...] = product(start, factor)
    ys[...] = factor

    def newton(i, carry):
        upper = xs[...]
        lower = ys[...]
        factor = 1.5 * identity - 0.5 * product(lower, upper)
        xs[...] = product(upper, factor)
        ys[...] = product(factor, lower)
        return carry

    lax.fori_loop(1, ITERS, newton, 0)
    root = ys[...] / jnp.sqrt(trace)
    spun = product(root, deviation)
    half_step = product(coupling, root)
    shift = product(half_step, spun)[0:1] * (1.0 / math.sqrt(members - 1))
    result = spun + (center + shift)
    for m in range(2):
        for f in range(2):
            for half in range(2):
                column = (f * 2 + half) * 128
                xf[pl.ds(m * 4 + half * 2 + f, rows, stride=8), :] = result[
                    m * rows : (m + 1) * rows, column : column + 128
                ]
    s2buf[...] = xf[...].reshape(rows, 8, 128).astype(BF)
    swap_slabs(s2buf, out, ssem2, rsem2)


def per_device(rows, lats, background, wind_east, wind_north, obs_index, obs_value, obs_scale):
    members = 2 * rows
    total = rows + 2 * HALO
    bg = background.reshape(rows, 2, 2, 2, 128).transpose(0, 1, 3, 2, 4).reshape(rows, 8, 128)
    anywhere = pl.BlockSpec(memory_space=pl.ANY)
    vmem = pl.BlockSpec(memory_space=pltpu.VMEM)
    wide = pltpu.VMEM((total, 8, 128), F32)
    grid_wind = pltpu.VMEM((total, 256), F32)
    slabs = pltpu.VMEM((rows, 8, 128), BF)
    block = pltpu.VMEM((members + 16, NOBS), BF)
    square = pltpu.VMEM((members, members), F32)
    dma = pltpu.SemaphoreType.DMA
    out = pl.pallas_call(
        functools.partial(main_kernel, rows, lats),
        out_shape=jax.ShapeDtypeStruct((rows, 8, 128), BF),
        in_specs=[anywhere] * 6,
        out_specs=anywhere,
        scratch_shapes=[
            pltpu.VMEM((rows, 8, 128), F32), pltpu.VMEM((rows, 256), BF), pltpu.VMEM((rows, 256), BF),
            pltpu.VMEM((1, NOBS), jnp.int32), pltpu.VMEM((1, NOBS), F32), pltpu.VMEM((1, NOBS), F32),
            pltpu.VMEM((HALO, 8, 128), F32), pltpu.VMEM((HALO, 8, 128), F32),
            *[pltpu.VMEM((HALO, 256), BF)] * 4,
            pltpu.VMEM((4 * STEPS + 1, total, 8, 128), F32), wide, wide, grid_wind, grid_wind,
            pltpu.VMEM((rows, 8, 128), I16), pltpu.VMEM((rows, 8, 128), I16),
            pltpu.VMEM((8 * rows, 128), F32), block, block, block,
            square, square, slabs,
            dma((6,)), dma((6,)), dma((6,)), pltpu.SemaphoreType.REGULAR((8,)),
            dma((rows,)), dma((rows,)), dma((2,)), dma((2,)), dma((rows,)), dma((rows,)),
        ],
        compiler_params=pltpu.CompilerParams(collective_id=0, has_side_effects=True),
        name="main",
    )(
        bg, wind_east, wind_north,
        obs_index.reshape(1, NOBS), obs_value.reshape(1, NOBS), obs_scale.reshape(1, NOBS),
    )
    out = out.astype(F32)
    return out.reshape(rows, 2, 2, 2, 128).transpose(0, 1, 3, 2, 4).reshape(rows, 2, 2, 256)


def solution(mesh):
    in_specs = (
        P("lat", "mem", None, None),
        P("lat", None),
        P("lat", None),
        P("lat", "mem", None, None),
        P("lat", "mem", None, None),
        P("lat", "mem", None, None),
    )
    return jax.shard_map(
        functools.partial(per_device, mesh.shape["mem"], mesh.shape["lat"]),
        mesh=mesh,
        in_specs=in_specs,
        out_specs=P("lat", "mem", None, None),
        check_vma=False,
    )
```

```python
import functools
import math

import jax
import jax.numpy as jnp
from jax import lax
from jax.experimental import pallas as pl
from jax.experimental.pallas import tpu as pltpu
from jax.sharding import PartitionSpec as P

PW = 256
NOBS = 128
STEPS = 4
ITERS = 12
HALO = 4 * STEPS
CHUNK = HALO
BOUND = 18432.0
LEVELS = 32760.0
FINE = 16384.0
SPAN = math.log(1.0 + BOUND * FINE)
I16 = jnp.int16
I32 = jnp.int32
MESH = pl.DeviceIdType.MESH
BF = jnp.bfloat16
F32 = jnp.float32


def remote(src, dst, send, recv, lat, mem):
    return pltpu.make_async_remote_copy(
        src_ref=src,
        dst_ref=dst,
        send_sem=send,
        recv_sem=recv,
        device_id={"lat": lat, "mem": mem},
        device_id_type=MESH,
    )


def signal(sem, lat, mem):
    pl.semaphore_signal(
        sem, inc=1, device_id={"lat": lat, "mem": mem}, device_id_type=MESH
    )


def swap_middle(x):
    sub = lax.broadcasted_iota(jnp.int32, x.shape, 1)
    down = pltpu.roll(x, 2, 1)
    lift = pltpu.roll(x, 6, 1)
    return jnp.where(
        (sub == 4) | (sub == 5), down, jnp.where((sub == 2) | (sub == 3), lift, x)
    )


def halves(x):
    high = x.astype(BF)
    low = (x - high.astype(F32)).astype(BF)
    return high, low


def dot(a, b):
    return lax.dot_general(a, b, (((1,), (0,)), ((), ())), preferred_element_type=F32)


def dot_nt(a, b):
    return lax.dot_general(a, b, (((1,), (1,)), ((), ())), preferred_element_type=F32)


def product(a, b):
    n = b.shape[1]
    ah, al = halves(a)
    bh, bl = halves(b)
    right = jnp.concatenate([bh, bl], axis=1)
    both = dot(jnp.concatenate([ah, al], axis=1), jnp.concatenate([right, right], axis=0))
    return both[:, :n] + both[:, n:]


def encode(x):
    level = jnp.log(1.0 + jnp.abs(x) * FINE) * (LEVELS / SPAN)
    level = jnp.round(level).astype(I32)
    return jnp.where(x < 0.0, -level, level).astype(I16)


def decode(coded):
    level = coded.astype(I32).astype(F32)
    size = (jnp.exp(jnp.abs(level) * (SPAN / LEVELS)) - 1.0) * (1.0 / FINE)
    return jnp.where(level < 0.0, -size, size)


def main_kernel(
    rows, lats,
    bg_in, we_in, wn_in, idx_in, val_in, scl_in,
    out,
    bg, we, wn, idx, val, scl, up, dn, weu, wed, wnu, wnd,
    t, we8, wn8, wfe, wfn, sbuf, rbuf, xf, bext, ub, db, xs, ys, s2buf,
    lsem, hsend, hrecv, rounds, ssem1, rsem1, ssemn, rsemn, ssem2, rsem2,
):
    members = 2 * rows
    total = rows + 2 * HALO
    lat = lax.axis_index("lat")
    mem = lax.axis_index("mem")
    place = lat * rows + mem
    last_place = lats * rows - 1
    has_prev = place > 0
    has_next = place < last_place
    prev_place = jnp.maximum(place - 1, 0)
    next_place = jnp.minimum(place + 1, last_place)
    prev_at = (prev_place // rows, prev_place % rows)
    next_at = (next_place // rows, next_place % rows)
    barrier = pltpu.get_barrier_semaphore()
    edge_prev = jnp.logical_and(mem == 0, lat > 0)
    edge_next = jnp.logical_and(mem == rows - 1, lat < lats - 1)

    zs = rows // 4
    core = mem % 2
    z_here = (mem // 2) % zs
    column = mem // (rows // 2)
    starts = [
        ((column + dx) % 2) * (rows // 2) + (core + dc) % 2 for dx, dc in ((1, 1), (1, 0), (0, 1), (0, 0))
    ]

    def for_peers(act):
        def visit(z, count):
            twice = 2 * jnp.where(z >= zs, z - zs, z)
            for start in starts[:count]:
                act(start + twice)

        def pair(j, carry):
            visit(z_here + (zs // 2 - j), 4)
            visit(z_here + (zs // 2 + 1 + j), 4)
            return carry

        lax.fori_loop(0, zs // 2 - 1, pair, 0)
        visit(z_here + 1, 4)
        visit(z_here, 3)

    has_up = lat > 0
    has_dn = lat < lats - 1

    def place_at(dx, dz, dc):
        col = (column + dx) % 2
        return col * (rows // 2) + ((z_here + dz + zs) % zs) * 2 + (core + dc) % 2

    first_reach = 1
    near_by = [
        (dx, dz, dc)
        for dz in range(-first_reach, first_reach + 1)
        for dx in range(2)
        for dc in range(2)
        if (dx, dz, dc) != (0, 0, 0)
    ]
    for near in near_by:
        signal(barrier, lat, place_at(*near))

    @pl.when(has_up)
    def _():
        signal(barrier, lat - 1, mem)

    @pl.when(has_dn)
    def _():
        signal(barrier, lat + 1, mem)

    @pl.when(edge_prev)
    def _():
        signal(barrier, *prev_at)

    @pl.when(edge_next)
    def _():
        signal(barrier, *next_at)

    local = [
        pltpu.make_async_copy(src, dst, lsem.at[i])
        for i, (src, dst) in enumerate(
            ((bg_in, bg), (we_in, we), (wn_in, wn), (idx_in, idx), (val_in, val), (scl_in, scl))
        )
    ]
    for copy in local:
        copy.start()
    greeted = len(near_by)
    for more in (has_up, has_dn, edge_prev, edge_next):
        greeted = greeted + more.astype(jnp.int32)
    pl.semaphore_wait(barrier, greeted)

    first = pl.ds(0, HALO)
    last = pl.ds(rows - HALO, HALO)

    def edge_copies(target, at, sinks, base):
        return [
            remote(src.at[at], dst, hsend.at[base + i], hrecv.at[base + i], target, mem)
            for i, (src, dst) in enumerate(zip((bg_in, we_in, wn_in), sinks))
        ]

    to_up = edge_copies(lat - 1, first, (dn, wed, wnd), 0)
    to_dn = edge_copies(lat + 1, last, (up, weu, wnu), 3)

    @pl.when(has_up)
    def _():
        for copy in to_up:
            copy.start()

    @pl.when(has_dn)
    def _():
        for copy in to_dn:
            copy.start()

    turns = []
    reach = first_reach
    while reach < zs // 2:
        turns.append(((0, reach, 0), (0, -reach, 0)))
        reach *= 2

    def tell(turn):
        for near in turns[turn]:
            signal(rounds.at[turn], lat, place_at(*near))

    def hear(turn):
        pl.semaphore_wait(rounds.at[turn], len(turns[turn]))

    if turns:
        tell(0)
    for copy in local:
        copy.wait()

    for c in range(rows // 8):
        t[0, HALO + 8 * c : HALO + 8 * c + 8] = swap_middle(bg[8 * c : 8 * c + 8])
    low_half = lax.broadcasted_iota(jnp.int32, (8, 128), 0) < 4

    def spread_wind(wf, w8, start, stop):
        def widen(c, carry):
            for r in range(8):
                row = wf[pl.ds(8 * c + r, 1), :]
                w8[8 * c + r] = jnp.where(
                    low_half,
                    jnp.broadcast_to(row[:, :128], (8, 128)),
                    jnp.broadcast_to(row[:, 128:], (8, 128)),
                )
            return carry

        lax.fori_loop(start // 8, stop // 8, widen, 0)

    for wmid, w8, buf in ((we, we8, wfe), (wn, wn8, wfn)):
        buf[HALO : HALO + rows] = wmid[...].astype(F32) * -0.5
        spread_wind(buf, w8, HALO, HALO + rows)
    lane = lax.broadcasted_iota(jnp.int32, (CHUNK, 8, 128), 2)

    def staged(s, base, start, scale):
        block = t[s - 1, pl.ds(start - 1, CHUNK + 2)]
        mid = block[1 : CHUNK + 1]
        other = pltpu.roll(mid, 4, 1)
        nxt = pltpu.roll(jnp.where(lane == 0, other, mid), 127, 2)
        prv = pltpu.roll(jnp.where(lane == 127, other, mid), 1, 2)
        here = pl.ds(start, CHUNK)
        slope = we8[here] * (nxt - prv) + wn8[here] * (block[2 : CHUNK + 2] - block[0:CHUNK])
        return t[base, here] + (slope if scale == 1.0 else scale * slope)

    def inner_step(i, carry):
        for k in range(4):
            s = 4 * i + k + 1

            def chunk(c, carry, s=s, k=k):
                start = HALO + s + CHUNK * c
                t[s, pl.ds(start, CHUNK)] = staged(s, 4 * i, start, 1.0 / (4 - k))
                return carry

            lax.fori_loop(0, (rows - 2 * s + CHUNK - 1) // CHUNK, chunk, 0)
        return carry

    heard = 0
    done = 0
    while heard < len(turns) - 1:
        hear(heard)
        heard += 1
        tell(heard)
        lax.fori_loop(done, done + 2 if done < STEPS else done, inner_step, 0)
        done = min(done + 2, STEPS)
    lax.fori_loop(done, STEPS, inner_step, 0)

    def pack(start, stop):
        def some(c, carry):
            sbuf[pl.ds(CHUNK * c, CHUNK)] = encode(t[4 * STEPS, pl.ds(HALO + CHUNK * c, CHUNK)])
            return carry

        lax.fori_loop(start // CHUNK, stop // CHUNK, some, 0)

    if rows > 2 * HALO:
        pack(HALO, rows - HALO)

    @pl.when(has_up)
    def _():
        for copy in to_up:
            copy.wait_send()
        for copy in to_dn:
            copy.wait_recv()

    @pl.when(has_dn)
    def _():
        for copy in to_dn:
            copy.wait_send()
        for copy in to_up:
            copy.wait_recv()

    for west, weast, w8, buf in ((weu, wed, we8, wfe), (wnu, wnd, wn8, wfn)):
        buf[0:HALO] = jnp.where(has_up, west[...].astype(F32), 0.0) * -0.5
        buf[HALO + rows : total] = jnp.where(has_dn, weast[...].astype(F32), 0.0) * -0.5
        spread_wind(buf, w8, 0, HALO)
        spread_wind(buf, w8, HALO + rows, total)
    for c in range(HALO // 8):
        at = slice(8 * c, 8 * c + 8)
        t[0, at] = jnp.where(has_up, swap_middle(up[at]), 0.0)
        below = HALO + rows + 8 * c
        t[0, below : below + 8] = jnp.where(has_dn, swap_middle(dn[at]), 0.0)

    def rim_step(i, carry):
        for k in range(4):
            s = 4 * i + k + 1
            low = staged(s, 4 * i, s, 1.0 / (4 - k))
            high = staged(s, 4 * i, total - CHUNK - s, 1.0 / (4 - k))
            t[s, pl.ds(s, CHUNK)] = low
            t[s, pl.ds(total - CHUNK - s, CHUNK)] = high
        return carry

    lax.fori_loop(0, STEPS, rim_step, 0)
    if rows > 2 * HALO:
        pack(0, HALO)
        pack(rows - HALO, rows)
    else:
        pack(0, rows)
    if turns:
        hear(len(turns) - 1)

    def swap_slabs(source, sink, ssem, rsem):
        def send(to):
            remote(source.at[to], sink.at[mem], ssem.at[to], rsem.at[mem], lat, to).start()

        def settle(peer):
            remote(source.at[peer], sink.at[peer], ssem.at[peer], rsem.at[peer], lat, peer).wait()

        for_peers(send)
        own = pltpu.make_async_copy(source.at[mem], sink.at[mem], lsem.at[0])
        own.start()
        own.wait()
        for_peers(settle)

    swap_slabs(sbuf, rbuf, ssem1, rsem1)

    xf[...] = decode(rbuf[...]).reshape(8 * rows, 128)
    parts = [
        jnp.concatenate(
            [xf[pl.ds(half * 4 + m * 2 + f, rows, stride=8), :] for f in range(2) for half in range(2)],
            axis=1,
        )
        for m in range(2)
    ]
    x = jnp.concatenate(parts, axis=0)
    ids = lax.broadcasted_iota(jnp.int32, (2 * PW, NOBS), 0)
    selector = jnp.where(ids == idx[...], 1.0, 0.0).astype(BF)
    xh = x.astype(BF)
    rest = x - xh.astype(F32)
    xm, xl = halves(rest)
    pieces = dot(jnp.concatenate([xh, xm, xl], axis=0), selector)
    projected = pieces[:members] + (
        pieces[members : 2 * members] + pieces[2 * members : 3 * members]
    )
    average = jnp.sum(projected, axis=0, keepdims=True) * (1.0 / members)
    spread = (projected - average) * (scl[...] * (1.0 / math.sqrt(members - 1)))
    innovation = (val[...] - average) * scl[...]
    bext[0:members] = spread.astype(BF)
    first = lax.broadcasted_iota(jnp.int32, (16, NOBS), 0) == 0
    bext[members : members + 16] = jnp.where(
        first, jnp.broadcast_to(innovation, (16, NOBS)), 0.0
    ).astype(BF)

    to_next = remote(bext, ub, ssemn.at[0], rsemn.at[0], *next_at)
    to_prev = remote(bext, db, ssemn.at[1], rsemn.at[1], *prev_at)

    @pl.when(has_next)
    def _():
        to_next.start()

    @pl.when(has_prev)
    def _():
        to_prev.start()

    own = 3.0 * dot_nt(bext[...], bext[0:members])
    center = jnp.sum(x, axis=0, keepdims=True) * (1.0 / members)
    deviation = x - center

    @pl.when(jnp.logical_not(has_prev))
    def _():
        ub[...] = jnp.zeros_like(ub)

    @pl.when(jnp.logical_not(has_next))
    def _():
        db[...] = jnp.zeros_like(db)

    @pl.when(has_next)
    def _():
        to_next.wait_send()
        to_prev.wait_recv()

    @pl.when(has_prev)
    def _():
        to_prev.wait_send()
        to_next.wait_recv()

    gram = own + dot_nt(ub[...], ub[0:members]) + dot_nt(db[...], db[0:members])
    coupling = gram[members : members + 8]
    square = lax.broadcasted_iota(jnp.int32, (members, members), 0)
    identity = jnp.where(
        square == lax.broadcasted_iota(jnp.int32, (members, members), 1), 1.0, 0.0
    )
    system = gram[0:members] + identity
    trace = jnp.sum(
        jnp.sum(system * identity, axis=1, keepdims=True), axis=0, keepdims=True
    )
    start = system / trace
    factor = 1.5 * identity - 0.5 * start
    xs[...] = product(start, factor)
    ys[...] = factor

    def newton(i, carry):
        upper = xs[...]
        lower = ys[...]
        factor = 1.5 * identity - 0.5 * product(lower, upper)
        xs[...] = product(upper, factor)
        ys[...] = product(factor, lower)
        return carry

    lax.fori_loop(1, ITERS, newton, 0)
    root = ys[...] / jnp.sqrt(trace)
    spun = product(root, deviation)
    half_step = product(coupling, root)
    shift = product(half_step, spun)[0:1] * (1.0 / math.sqrt(members - 1))
    result = spun + (center + shift)
    for m in range(2):
        for f in range(2):
            for half in range(2):
                column = (f * 2 + half) * 128
                xf[pl.ds(m * 4 + half * 2 + f, rows, stride=8), :] = result[
                    m * rows : (m + 1) * rows, column : column + 128
                ]
    s2buf[...] = xf[...].reshape(rows, 8, 128).astype(BF)
    swap_slabs(s2buf, out, ssem2, rsem2)


def per_device(rows, lats, background, wind_east, wind_north, obs_index, obs_value, obs_scale):
    members = 2 * rows
    total = rows + 2 * HALO
    bg = background.reshape(rows, 2, 2, 2, 128).transpose(0, 1, 3, 2, 4).reshape(rows, 8, 128)
    anywhere = pl.BlockSpec(memory_space=pl.ANY)
    vmem = pl.BlockSpec(memory_space=pltpu.VMEM)
    wide = pltpu.VMEM((total, 8, 128), F32)
    grid_wind = pltpu.VMEM((total, 256), F32)
    slabs = pltpu.VMEM((rows, 8, 128), BF)
    block = pltpu.VMEM((members + 16, NOBS), BF)
    square = pltpu.VMEM((members, members), F32)
    dma = pltpu.SemaphoreType.DMA
    out = pl.pallas_call(
        functools.partial(main_kernel, rows, lats),
        out_shape=jax.ShapeDtypeStruct((rows, 8, 128), BF),
        in_specs=[anywhere] * 6,
        out_specs=anywhere,
        scratch_shapes=[
            pltpu.VMEM((rows, 8, 128), F32), pltpu.VMEM((rows, 256), BF), pltpu.VMEM((rows, 256), BF),
            pltpu.VMEM((1, NOBS), jnp.int32), pltpu.VMEM((1, NOBS), F32), pltpu.VMEM((1, NOBS), F32),
            pltpu.VMEM((HALO, 8, 128), F32), pltpu.VMEM((HALO, 8, 128), F32),
            *[pltpu.VMEM((HALO, 256), BF)] * 4,
            pltpu.VMEM((4 * STEPS + 1, total, 8, 128), F32), wide, wide, grid_wind, grid_wind,
            pltpu.VMEM((rows, 8, 128), I16), pltpu.VMEM((rows, 8, 128), I16),
            pltpu.VMEM((8 * rows, 128), F32), block, block, block,
            square, square, slabs,
            dma((6,)), dma((6,)), dma((6,)), pltpu.SemaphoreType.REGULAR((8,)),
            dma((rows,)), dma((rows,)), dma((2,)), dma((2,)), dma((rows,)), dma((rows,)),
        ],
        compiler_params=pltpu.CompilerParams(collective_id=0, has_side_effects=True),
        name="main",
    )(
        bg, wind_east, wind_north,
        obs_index.reshape(1, NOBS), obs_value.reshape(1, NOBS), obs_scale.reshape(1, NOBS),
    )
    out = out.astype(F32)
    return out.reshape(rows, 2, 2, 2, 128).transpose(0, 1, 3, 2, 4).reshape(rows, 2, 2, 256)


def solution(mesh):
    in_specs = (
        P("lat", "mem", None, None),
        P("lat", None),
        P("lat", None),
        P("lat", "mem", None, None),
        P("lat", "mem", None, None),
        P("lat", "mem", None, None),
    )
    return jax.shard_map(
        functools.partial(per_device, mesh.shape["mem"], mesh.shape["lat"]),
        mesh=mesh,
        in_specs=in_specs,
        out_specs=P("lat", "mem", None, None),
        check_vma=False,
    )
```

```python
import functools
import math

import jax
import jax.numpy as jnp
from jax import lax
from jax.experimental import pallas as pl
from jax.experimental.pallas import tpu as pltpu
from jax.sharding import PartitionSpec as P

PW = 256
NOBS = 128
STEPS = 4
ITERS = 12
HALO = 4 * STEPS
CHUNK = HALO
BOUND = 18432.0
LEVELS = 32760.0
FINE = 16384.0
SPAN = math.log(1.0 + BOUND * FINE)
I16 = jnp.int16
I32 = jnp.int32
MESH = pl.DeviceIdType.MESH
BF = jnp.bfloat16
F32 = jnp.float32


def remote(src, dst, send, recv, lat, mem):
    return pltpu.make_async_remote_copy(
        src_ref=src,
        dst_ref=dst,
        send_sem=send,
        recv_sem=recv,
        device_id={"lat": lat, "mem": mem},
        device_id_type=MESH,
    )


def signal(sem, lat, mem):
    pl.semaphore_signal(
        sem, inc=1, device_id={"lat": lat, "mem": mem}, device_id_type=MESH
    )


def swap_middle(x):
    sub = lax.broadcasted_iota(jnp.int32, x.shape, 1)
    down = pltpu.roll(x, 2, 1)
    lift = pltpu.roll(x, 6, 1)
    return jnp.where(
        (sub == 4) | (sub == 5), down, jnp.where((sub == 2) | (sub == 3), lift, x)
    )


def halves(x):
    high = x.astype(BF)
    low = (x - high.astype(F32)).astype(BF)
    return high, low


def dot(a, b):
    return lax.dot_general(a, b, (((1,), (0,)), ((), ())), preferred_element_type=F32)


def dot_nt(a, b):
    return lax.dot_general(a, b, (((1,), (1,)), ((), ())), preferred_element_type=F32)


def product(a, b):
    n = b.shape[1]
    ah, al = halves(a)
    bh, bl = halves(b)
    right = jnp.concatenate([bh, bl], axis=1)
    both = dot(jnp.concatenate([ah, al], axis=1), jnp.concatenate([right, right], axis=0))
    return both[:, :n] + both[:, n:]


def encode(x):
    level = jnp.log(1.0 + jnp.abs(x) * FINE) * (LEVELS / SPAN)
    level = jnp.round(level).astype(I32)
    return jnp.where(x < 0.0, -level, level).astype(I16)


def decode(coded):
    level = coded.astype(I32).astype(F32)
    size = (jnp.exp(jnp.abs(level) * (SPAN / LEVELS)) - 1.0) * (1.0 / FINE)
    return jnp.where(level < 0.0, -size, size)


def main_kernel(
    rows, lats,
    bg_in, we_in, wn_in, idx_in, val_in, scl_in,
    out,
    bg, we, wn, idx, val, scl, up, dn, weu, wed, wnu, wnd,
    t, we8, wn8, wfe, wfn, sbuf, rbuf, xf, bext, ub, db, xs, ys, s2buf,
    lsem, hsend, hrecv, rounds, ssem1, rsem1, ssemn, rsemn, ssem2, rsem2,
):
    members = 2 * rows
    total = rows + 2 * HALO
    lat = lax.axis_index("lat")
    mem = lax.axis_index("mem")
    place = lat * rows + mem
    last_place = lats * rows - 1
    has_prev = place > 0
    has_next = place < last_place
    prev_place = jnp.maximum(place - 1, 0)
    next_place = jnp.minimum(place + 1, last_place)
    prev_at = (prev_place // rows, prev_place % rows)
    next_at = (next_place // rows, next_place % rows)
    barrier = pltpu.get_barrier_semaphore()
    edge_prev = jnp.logical_and(mem == 0, lat > 0)
    edge_next = jnp.logical_and(mem == rows - 1, lat < lats - 1)

    zs = rows // 4
    core = mem % 2
    z_here = (mem // 2) % zs
    column = mem // (rows // 2)
    starts = [
        ((column + dx) % 2) * (rows // 2) + (core + dc) % 2 for dx, dc in ((1, 1), (1, 0), (0, 1), (0, 0))
    ]

    def for_peers(act):
        def visit(z, count):
            twice = 2 * jnp.where(z >= zs, z - zs, z)
            for start in starts[:count]:
                act(start + twice)

        def pair(j, carry):
            visit(z_here + (zs // 2 - j), 4)
            visit(z_here + (zs // 2 + 1 + j), 4)
            return carry

        lax.fori_loop(0, zs // 2 - 1, pair, 0)
        visit(z_here + 1, 4)
        visit(z_here, 3)

    has_up = lat > 0
    has_dn = lat < lats - 1

    def place_at(dx, dz, dc):
        col = (column + dx) % 2
        return col * (rows // 2) + ((z_here + dz + zs) % zs) * 2 + (core + dc) % 2

    first_reach = 1
    near_by = [
        (dx, dz, dc)
        for dz in range(-first_reach, first_reach + 1)
        for dx in range(2)
        for dc in range(2)
        if (dx, dz, dc) != (0, 0, 0)
    ]
    for near in near_by:
        signal(barrier, lat, place_at(*near))

    @pl.when(has_up)
    def _():
        signal(barrier, lat - 1, mem)

    @pl.when(has_dn)
    def _():
        signal(barrier, lat + 1, mem)

    @pl.when(edge_prev)
    def _():
        signal(barrier, *prev_at)

    @pl.when(edge_next)
    def _():
        signal(barrier, *next_at)

    local = [
        pltpu.make_async_copy(src, dst, lsem.at[i])
        for i, (src, dst) in enumerate(
            ((bg_in, bg), (we_in, we), (wn_in, wn), (idx_in, idx), (val_in, val), (scl_in, scl))
        )
    ]
    for copy in local:
        copy.start()
    greeted = len(near_by)
    for more in (has_up, has_dn, edge_prev, edge_next):
        greeted = greeted + more.astype(jnp.int32)
    pl.semaphore_wait(barrier, greeted)

    first = pl.ds(0, HALO)
    last = pl.ds(rows - HALO, HALO)

    def edge_copies(target, at, sinks, base):
        return [
            remote(src.at[at], dst, hsend.at[base + i], hrecv.at[base + i], target, mem)
            for i, (src, dst) in enumerate(zip((bg_in, we_in, wn_in), sinks))
        ]

    to_up = edge_copies(lat - 1, first, (dn, wed, wnd), 0)
    to_dn = edge_copies(lat + 1, last, (up, weu, wnu), 3)

    @pl.when(has_up)
    def _():
        for copy in to_up:
            copy.start()

    @pl.when(has_dn)
    def _():
        for copy in to_dn:
            copy.start()

    turns = []
    reach = first_reach
    while reach < zs // 2:
        turns.append(((0, reach, 0), (0, -reach, 0)))
        reach *= 2

    def tell(turn):
        for near in turns[turn]:
            signal(rounds.at[turn], lat, place_at(*near))

    def hear(turn):
        pl.semaphore_wait(rounds.at[turn], len(turns[turn]))

    if turns:
        tell(0)
    for copy in local:
        copy.wait()

    for c in range(rows // 8):
        t[0, HALO + 8 * c : HALO + 8 * c + 8] = swap_middle(bg[8 * c : 8 * c + 8])
    low_half = lax.broadcasted_iota(jnp.int32, (8, 128), 0) < 4

    def spread_wind(wf, w8, start, stop):
        def widen(c, carry):
            for r in range(CHUNK):
                row = wf[pl.ds(CHUNK * c + r, 1), :]
                w8[CHUNK * c + r] = jnp.where(
                    low_half,
                    jnp.broadcast_to(row[:, :128], (8, 128)),
                    jnp.broadcast_to(row[:, 128:], (8, 128)),
                )
            return carry

        lax.fori_loop(start // CHUNK, stop // CHUNK, widen, 0)

    for wmid, w8, buf in ((we, we8, wfe), (wn, wn8, wfn)):
        buf[HALO : HALO + rows] = wmid[...].astype(F32) * -0.5
        spread_wind(buf, w8, HALO, HALO + rows)
    lane = lax.broadcasted_iota(jnp.int32, (CHUNK, 8, 128), 2)

    def staged(s, base, start, scale):
        block = t[s - 1, pl.ds(start - 1, CHUNK + 2)]
        mid = block[1 : CHUNK + 1]
        other = pltpu.roll(mid, 4, 1)
        nxt = pltpu.roll(jnp.where(lane == 0, other, mid), 127, 2)
        prv = pltpu.roll(jnp.where(lane == 127, other, mid), 1, 2)
        here = pl.ds(start, CHUNK)
        slope = we8[here] * (nxt - prv) + wn8[here] * (block[2 : CHUNK + 2] - block[0:CHUNK])
        return t[base, here] + (slope if scale == 1.0 else scale * slope)

    def inner_step(i, carry):
        for k in range(4):
            s = 4 * i + k + 1

            def chunk(c, carry, s=s, k=k):
                start = HALO + s + CHUNK * c
                t[s, pl.ds(start, CHUNK)] = staged(s, 4 * i, start, 1.0 / (4 - k))
                return carry

            lax.fori_loop(0, (rows - 2 * s + CHUNK - 1) // CHUNK, chunk, 0)
        return carry

    heard = 0
    done = 0
    while heard < len(turns) - 1:
        hear(heard)
        heard += 1
        tell(heard)
        lax.fori_loop(done, done + 2 if done < STEPS else done, inner_step, 0)
        done = min(done + 2, STEPS)
    lax.fori_loop(done, STEPS, inner_step, 0)

    def pack(start, stop):
        def some(c, carry):
            sbuf[pl.ds(CHUNK * c, CHUNK)] = encode(t[4 * STEPS, pl.ds(HALO + CHUNK * c, CHUNK)])
            return carry

        lax.fori_loop(start // CHUNK, stop // CHUNK, some, 0)

    if rows > 2 * HALO:
        pack(HALO, rows - HALO)

    @pl.when(has_up)
    def _():
        for copy in to_up:
            copy.wait_send()
        for copy in to_dn:
            copy.wait_recv()

    @pl.when(has_dn)
    def _():
        for copy in to_dn:
            copy.wait_send()
        for copy in to_up:
            copy.wait_recv()

    for west, weast, w8, buf in ((weu, wed, we8, wfe), (wnu, wnd, wn8, wfn)):
        buf[0:HALO] = jnp.where(has_up, west[...].astype(F32), 0.0) * -0.5
        buf[HALO + rows : total] = jnp.where(has_dn, weast[...].astype(F32), 0.0) * -0.5
        spread_wind(buf, w8, 0, HALO)
        spread_wind(buf, w8, HALO + rows, total)
    for c in range(HALO // 8):
        at = slice(8 * c, 8 * c + 8)
        t[0, at] = jnp.where(has_up, swap_middle(up[at]), 0.0)
        below = HALO + rows + 8 * c
        t[0, below : below + 8] = jnp.where(has_dn, swap_middle(dn[at]), 0.0)

    def rim_step(i, carry):
        for k in range(4):
            s = 4 * i + k + 1
            low = staged(s, 4 * i, s, 1.0 / (4 - k))
            high = staged(s, 4 * i, total - CHUNK - s, 1.0 / (4 - k))
            t[s, pl.ds(s, CHUNK)] = low
            t[s, pl.ds(total - CHUNK - s, CHUNK)] = high
        return carry

    lax.fori_loop(0, STEPS, rim_step, 0)
    if rows > 2 * HALO:
        pack(0, HALO)
        pack(rows - HALO, rows)
    else:
        pack(0, rows)
    if turns:
        hear(len(turns) - 1)

    def swap_slabs(source, sink, ssem, rsem):
        def send(to):
            remote(source.at[to], sink.at[mem], ssem.at[to], rsem.at[mem], lat, to).start()

        def settle(peer):
            remote(source.at[peer], sink.at[peer], ssem.at[peer], rsem.at[peer], lat, peer).wait()

        for_peers(send)
        own = pltpu.make_async_copy(source.at[mem], sink.at[mem], lsem.at[0])
        own.start()
        own.wait()
        for_peers(settle)

    swap_slabs(sbuf, rbuf, ssem1, rsem1)

    xf[...] = decode(rbuf[...]).reshape(8 * rows, 128)
    parts = [
        jnp.concatenate(
            [xf[pl.ds(half * 4 + m * 2 + f, rows, stride=8), :] for f in range(2) for half in range(2)],
            axis=1,
        )
        for m in range(2)
    ]
    x = jnp.concatenate(parts, axis=0)
    ids = lax.broadcasted_iota(jnp.int32, (2 * PW, NOBS), 0)
    selector = jnp.where(ids == idx[...], 1.0, 0.0).astype(BF)
    xh = x.astype(BF)
    rest = x - xh.astype(F32)
    xm, xl = halves(rest)
    pieces = dot(jnp.concatenate([xh, xm, xl], axis=0), selector)
    projected = pieces[:members] + (
        pieces[members : 2 * members] + pieces[2 * members : 3 * members]
    )
    average = jnp.sum(projected, axis=0, keepdims=True) * (1.0 / members)
    spread = (projected - average) * (scl[...] * (1.0 / math.sqrt(members - 1)))
    innovation = (val[...] - average) * scl[...]
    bext[0:members] = spread.astype(BF)
    first = lax.broadcasted_iota(jnp.int32, (16, NOBS), 0) == 0
    bext[members : members + 16] = jnp.where(
        first, jnp.broadcast_to(innovation, (16, NOBS)), 0.0
    ).astype(BF)

    to_next = remote(bext, ub, ssemn.at[0], rsemn.at[0], *next_at)
    to_prev = remote(bext, db, ssemn.at[1], rsemn.at[1], *prev_at)

    @pl.when(has_next)
    def _():
        to_next.start()

    @pl.when(has_prev)
    def _():
        to_prev.start()

    own = 3.0 * dot_nt(bext[...], bext[0:members])
    center = jnp.sum(x, axis=0, keepdims=True) * (1.0 / members)
    deviation = x - center

    @pl.when(jnp.logical_not(has_prev))
    def _():
        ub[...] = jnp.zeros_like(ub)

    @pl.when(jnp.logical_not(has_next))
    def _():
        db[...] = jnp.zeros_like(db)

    @pl.when(has_next)
    def _():
        to_next.wait_send()
        to_prev.wait_recv()

    @pl.when(has_prev)
    def _():
        to_prev.wait_send()
        to_next.wait_recv()

    gram = own + dot_nt(ub[...], ub[0:members]) + dot_nt(db[...], db[0:members])
    coupling = gram[members : members + 8]
    square = lax.broadcasted_iota(jnp.int32, (members, members), 0)
    identity = jnp.where(
        square == lax.broadcasted_iota(jnp.int32, (members, members), 1), 1.0, 0.0
    )
    system = gram[0:members] + identity
    trace = jnp.sum(
        jnp.sum(system * identity, axis=1, keepdims=True), axis=0, keepdims=True
    )
    start = system / trace
    factor = 1.5 * identity - 0.5 * start
    xs[...] = product(start, factor)
    ys[...] = factor

    def newton(i, carry):
        upper = xs[...]
        lower = ys[...]
        factor = 1.5 * identity - 0.5 * product(lower, upper)
        xs[...] = product(upper, factor)
        ys[...] = product(factor, lower)
        return carry

    lax.fori_loop(1, ITERS, newton, 0)
    root = ys[...] / jnp.sqrt(trace)
    spun = product(root, deviation)
    half_step = product(coupling, root)
    shift = product(half_step, spun)[0:1] * (1.0 / math.sqrt(members - 1))
    result = spun + (center + shift)
    for m in range(2):
        for f in range(2):
            for half in range(2):
                column = (f * 2 + half) * 128
                xf[pl.ds(m * 4 + half * 2 + f, rows, stride=8), :] = result[
                    m * rows : (m + 1) * rows, column : column + 128
                ]
    s2buf[...] = xf[...].reshape(rows, 8, 128).astype(BF)
    swap_slabs(s2buf, out, ssem2, rsem2)


def per_device(rows, lats, background, wind_east, wind_north, obs_index, obs_value, obs_scale):
    members = 2 * rows
    total = rows + 2 * HALO
    bg = background.reshape(rows, 2, 2, 2, 128).transpose(0, 1, 3, 2, 4).reshape(rows, 8, 128)
    anywhere = pl.BlockSpec(memory_space=pl.ANY)
    vmem = pl.BlockSpec(memory_space=pltpu.VMEM)
    wide = pltpu.VMEM((total, 8, 128), F32)
    grid_wind = pltpu.VMEM((total, 256), F32)
    slabs = pltpu.VMEM((rows, 8, 128), BF)
    block = pltpu.VMEM((members + 16, NOBS), BF)
    square = pltpu.VMEM((members, members), F32)
    dma = pltpu.SemaphoreType.DMA
    out = pl.pallas_call(
        functools.partial(main_kernel, rows, lats),
        out_shape=jax.ShapeDtypeStruct((rows, 8, 128), BF),
        in_specs=[anywhere] * 6,
        out_specs=anywhere,
        scratch_shapes=[
            pltpu.VMEM((rows, 8, 128), F32), pltpu.VMEM((rows, 256), BF), pltpu.VMEM((rows, 256), BF),
            pltpu.VMEM((1, NOBS), jnp.int32), pltpu.VMEM((1, NOBS), F32), pltpu.VMEM((1, NOBS), F32),
            pltpu.VMEM((HALO, 8, 128), F32), pltpu.VMEM((HALO, 8, 128), F32),
            *[pltpu.VMEM((HALO, 256), BF)] * 4,
            pltpu.VMEM((4 * STEPS + 1, total, 8, 128), F32), wide, wide, grid_wind, grid_wind,
            pltpu.VMEM((rows, 8, 128), I16), pltpu.VMEM((rows, 8, 128), I16),
            pltpu.VMEM((8 * rows, 128), F32), block, block, block,
            square, square, slabs,
            dma((6,)), dma((6,)), dma((6,)), pltpu.SemaphoreType.REGULAR((8,)),
            dma((rows,)), dma((rows,)), dma((2,)), dma((2,)), dma((rows,)), dma((rows,)),
        ],
        compiler_params=pltpu.CompilerParams(collective_id=0, has_side_effects=True),
        name="main",
    )(
        bg, wind_east, wind_north,
        obs_index.reshape(1, NOBS), obs_value.reshape(1, NOBS), obs_scale.reshape(1, NOBS),
    )
    out = out.astype(F32)
    return out.reshape(rows, 2, 2, 2, 128).transpose(0, 1, 3, 2, 4).reshape(rows, 2, 2, 256)


def solution(mesh):
    in_specs = (
        P("lat", "mem", None, None),
        P("lat", None),
        P("lat", None),
        P("lat", "mem", None, None),
        P("lat", "mem", None, None),
        P("lat", "mem", None, None),
    )
    return jax.shard_map(
        functools.partial(per_device, mesh.shape["mem"], mesh.shape["lat"]),
        mesh=mesh,
        in_specs=in_specs,
        out_specs=P("lat", "mem", None, None),
        check_vma=False,
    )
```
